512 devices in a mesh: cell: 512 (over x, z, y, core).
Axes of the slice: x: 4, y: 8, z: 8, core: 2. Of those that a mesh axis runs over, the one named last changes fastest.
Arguments:
- features: bfloat16 [131072, 512], P('cell'), may hold values from -6 to 6
- radial: bfloat16 [131072, 8, 128], P('cell'), may hold values from 0 to 1
- neighbours: int32 [131072, 8], P('cell'), may hold values from 0 to 131071, as said below
- counts: int32 [131072], P('cell'), may hold values from 1 to 8, as said below
- cotangent: bfloat16 [131072, 8, 256], P('cell'), may hold values from -6 to 6
- w_self: bfloat16 [512, 512], replicated, may hold values from -0.25 to 0.25
- w_neighbour: bfloat16 [512, 512], replicated, may hold values from -0.25 to 0.25
- w_radial: bfloat16 [128, 512], replicated, may hold values from -0.5 to 0.5
- w_block: bfloat16 [512, 256], replicated, may hold values from -0.25 to 0.25
Outputs:
- blocks: bfloat16 [131072, 8, 256], P('cell')
- feat_grad: bfloat16 [131072, 512], P('cell')
The draws below stay inside these ranges and needn't reach their ends.
Inputs may be any that keep to these rules, and one draw needn't show every extreme that they name: `neighbours`: each neighbour index differs from its atom's index by 1 to 128. Only the first counts[i] slots of atom i are live, the rest are padding.
All inputs are finite; a program needn't handle non-finite values.
Results may differ from the reference program's by a relative error of at most 0.013.
Values may be sent and summed in bfloat16 or wider, within the bound.
A program may use at most 64 MiB of HBM per device.

```python
import jax
import jax.numpy as jnp
from jax import lax

F = 512
NR = 128
OB = 256
K = 8
AT_DEV = 256
HALO = 128
ATOMS = 131072
N_CELL = 512


def draw_neighbours(key, part):
    key_offset, key_sign = jax.random.split(jax.random.fold_in(key, 11))
    offsets = jax.random.randint(key_offset, (ATOMS, K), 1, HALO + 1)
    signs = jax.random.randint(key_sign, (ATOMS, K), 0, 2) * 2 - 1
    atom_index = jnp.arange(ATOMS, dtype=jnp.int32)[:, None]
    target = atom_index + signs * offsets
    flipped = atom_index - signs * offsets
    target = jnp.where((target < 0) | (target >= ATOMS), flipped, target)
    target = target.at[ATOMS - 2, 0].set(ATOMS - 1)
    target = target.at[1, 0].set(0)
    return target.astype(jnp.int32)


def draw_counts(key, part):
    key_level, key_count = jax.random.split(jax.random.fold_in(key, 23))
    domain_total = ATOMS // AT_DEV
    levels = jax.random.randint(key_level, (domain_total,), 1, K + 1)
    lowest = levels[jnp.arange(ATOMS, dtype=jnp.int32) // AT_DEV]
    spread = jax.random.randint(key_count, (ATOMS,), 0, K + 1)
    result = lowest + spread % (K + 1 - lowest)
    result = result.at[0].set(K)
    result = result.at[1].set(1)
    return result.astype(jnp.int32)


def block_scale(key, extent, cuts, least, top_value):
    level, own = 1.0, jax.random.fold_in(key, 6)
    for position, parts in cuts:
        steps = jnp.exp(jax.random.uniform(jax.random.fold_in(own, position), (parts,), jnp.float32, least / len(cuts), top_value / len(cuts)))
        level = level * jnp.repeat(steps, extent[position] // parts).reshape([-1 if axis == position else 1 for axis in range(len(extent))])
    return level


def normal_values(stream_key, dims, width, reach, cuts=(), kind=jnp.bfloat16):
    loudness = block_scale(stream_key, dims, cuts, -0.22, 0.18) if cuts else 1.0
    array = jax.random.normal(stream_key, dims, jnp.float32) * width * loudness
    return jnp.minimum(jnp.maximum(array, -reach), reach).astype(kind)


def setup_inputs(seed: int = 0) -> dict:
    key_list = jax.random.split(jax.random.key(seed), 10)
    features = normal_values(key_list[0], (ATOMS, F), 1.0, 6.0, ((0, 512),))
    radial = jnp.clip(1.0 * jax.random.uniform(key_list[1], (ATOMS, K, NR), jnp.float32) ** block_scale(key_list[1], (ATOMS, K, NR), ((0, 512),), -0.2, 0.2), 0.0, 1.0).astype(jnp.bfloat16)
    neighbours = draw_neighbours(jax.random.fold_in(key_list[9], 71), 0)
    counts = draw_counts(jax.random.fold_in(key_list[9], 71), 0)
    cotangent = normal_values(key_list[4], (ATOMS, K, OB), 1.0, 6.0, ((0, 512),))
    w_self = normal_values(key_list[5], (F, F), F ** -0.5, 0.25)
    w_neighbour = normal_values(key_list[6], (F, F), F ** -0.5, 0.25)
    w_radial = normal_values(key_list[7], (NR, F), NR ** -0.5, 0.5)
    w_block = normal_values(key_list[8], (F, OB), F ** -0.5, 0.25)
    return dict(features=features, radial=radial, neighbours=neighbours, counts=counts, cotangent=cotangent, w_self=w_self, w_neighbour=w_neighbour, w_radial=w_radial, w_block=w_block)


def reference(features, radial, neighbours, counts, cotangent, w_self, w_neighbour, w_radial, w_block):
    self_proj = jnp.dot(features, w_self, preferred_element_type=jnp.float32).astype(jnp.bfloat16)
    nbr_proj = jnp.dot(features, w_neighbour, preferred_element_type=jnp.float32).astype(jnp.bfloat16)
    slot_index = jnp.arange(K, dtype=jnp.int32)

    def block_step(carry, index):
        start = (index * AT_DEV).astype(jnp.int32)
        nbr_rows = lax.dynamic_slice_in_dim(neighbours, start, AT_DEV, 0).reshape(-1)
        radial_rows = lax.dynamic_slice_in_dim(radial, start, AT_DEV, 0).reshape(-1, NR)
        count_rows = lax.dynamic_slice_in_dim(counts, start, AT_DEV, 0)
        cotan_rows = lax.dynamic_slice_in_dim(cotangent, start, AT_DEV, 0).reshape(-1, OB)
        self_rows = lax.dynamic_slice_in_dim(self_proj, start, AT_DEV, 0)
        live_mask = (slot_index[None, :] < count_rows[:, None]).astype(jnp.float32)[:, :, None]
        radial_gate = jnp.dot(radial_rows, w_radial, preferred_element_type=jnp.float32).reshape(AT_DEV, K, F)
        gathered = nbr_proj[nbr_rows].reshape(AT_DEV, K, F)
        pre_act = (self_rows.astype(jnp.float32)[:, None, :] + gathered.astype(jnp.float32)) * radial_gate
        message = (jax.nn.silu(pre_act) * live_mask).astype(jnp.bfloat16)
        block_out = jnp.dot(message.reshape(-1, F), w_block, preferred_element_type=jnp.float32).astype(jnp.bfloat16)
        d_message = jnp.dot(cotan_rows, w_block.T, preferred_element_type=jnp.float32).reshape(AT_DEV, K, F)
        sigmoid_val = jax.nn.sigmoid(pre_act)
        adjoint = d_message * live_mask * (sigmoid_val * (1.0 + pre_act * (1.0 - sigmoid_val))) * radial_gate
        self_adj = jnp.sum(adjoint, axis=1)
        carry = carry.at[nbr_rows].add(adjoint.reshape(-1, F))
        return carry, (block_out.reshape(AT_DEV, K, OB), self_adj)

    summed, (block_parts, self_parts) = lax.scan(block_step, jnp.zeros((ATOMS, F), jnp.float32), jnp.arange(N_CELL, dtype=jnp.int32))
    blocks = block_parts.reshape(ATOMS, K, OB)
    self_adj = self_parts.reshape(ATOMS, F).astype(jnp.bfloat16)
    nbr_adj = summed.astype(jnp.bfloat16)
    feat_grad = jnp.dot(self_adj, w_self.T, preferred_element_type=jnp.float32) + jnp.dot(nbr_adj, w_neighbour.T, preferred_element_type=jnp.float32)
    return blocks, feat_grad.astype(jnp.bfloat16)
```

```python
import functools

import jax
import jax.numpy as jnp
from jax import lax
from jax.experimental import pallas as pl
from jax.experimental.pallas import tpu as pltpu
from jax.sharding import PartitionSpec as P

MESH = pl.DeviceIdType.MESH
BF = jnp.bfloat16
F32 = jnp.float32
DEAD = 1024.0
NT = (((1,), (1,)), ((), ()))


def dot(a, b):
    return jnp.dot(a, b, preferred_element_type=F32)


def dot_nt(a, b):
    return lax.dot_general(a, b, NT, preferred_element_type=F32)


def hot(mask):
    return jnp.where(mask, 1.0, 0.0).astype(BF)


def kernel(
    n_dev, slots, half, chunk,
    feat_hbm, rad_hbm, nbr_hbm, cnt_hbm, cot_hbm, ws_hbm, wn_hbm, wr_hbm, wb_hbm,
    blk_hbm, fg_hbm,
    feat, rad, nbr, cnt, cot, ws, wn, wr, wb,
    halo, rim_out, rim_in, own_proj, mix, p_own, p_rim, pt_own, pt_rim,
    gate, had, u_own, msg, adj, blk, own_sum, self_adj, fg_self, fg,
    in_sem, halo_send, halo_recv, rim_send, rim_recv, blk_sem, fg_sem,
):
    me = lax.axis_index("cell")
    right, left = lax.rem(me + 1, n_dev), lax.rem(me + n_dev - 1, n_dev)
    edges = half * slots

    barrier = pltpu.get_barrier_semaphore()
    for other in (left, right):
        pl.semaphore_signal(barrier, inc=1, device_id=(other,), device_id_type=MESH)

    pairs = [(nbr_hbm, nbr), (cnt_hbm, cnt), (feat_hbm, feat), (wn_hbm, wn), (ws_hbm, ws),
             (rad_hbm, rad), (wr_hbm, wr), (cot_hbm, cot), (wb_hbm, wb)]
    loads = [pltpu.make_async_copy(s, d, in_sem.at[i]) for i, (s, d) in enumerate(pairs)]
    for load in loads:
        load.start()

    pl.semaphore_wait(barrier, 2)
    halo_copies = [
        pltpu.make_async_remote_copy(
            src_ref=feat_hbm.at[pl.ds((1 - side) * half, half)], dst_ref=halo.at[side],
            send_sem=halo_send.at[side], recv_sem=halo_recv.at[side],
            device_id=((right, left)[side],), device_id_type=MESH)
        for side in (0, 1)
    ]
    for copy in halo_copies:
        copy.start()

    loads[0].wait()
    loads[1].wait()
    e_row = lax.broadcasted_iota(jnp.int32, (edges, half), 0)
    lane = lax.broadcasted_iota(jnp.int32, (edges, half), 1)
    spread = hot((e_row // slots) == lane)
    slot_of = lax.broadcasted_iota(jnp.int32, (slots, edges), 1)
    atom_lane = (slot_of // slots).astype(F32)
    slot_of = slot_of % slots
    slot_sub = lax.broadcasted_iota(jnp.int32, (slots, edges), 0)
    slot_pick = slot_of == slot_sub
    for h in (0, 1):
        ids = nbr[:, h * half:(h + 1) * half]
        shape = (slots, half)
        base = me * (2 * half) + h * half
        diff = ids - base - lax.broadcasted_iota(jnp.int32, shape, 1)
        live = lax.broadcasted_iota(jnp.int32, shape, 0) < cnt[:, h * half:(h + 1) * half]
        diff = jnp.where(live, diff.astype(F32), DEAD).astype(BF)
        z = jnp.where(slot_pick, dot_nt(diff, spread), 0.0)
        row = jnp.sum(z, axis=0, keepdims=True)
        row_t = row + atom_lane[:1] + half
        row_self = jnp.where(row < DEAD / 2, atom_lane[:1], -1.0)
        own_js = (1, 2) if h == 0 else (0, 1)
        rim_j = 0 if h == 0 else 2
        for c in range(0, edges, chunk):
            sub = lax.broadcasted_iota(jnp.int32, (half, chunk), 0).astype(F32)
            rt = row_t[:, c:c + chunk]
            rs = row_self[:, c:c + chunk]
            for pos, j in enumerate(own_js):
                pt_own[pos * half:(pos + 1) * half, h * edges + c:h * edges + c + chunk] = hot(
                    sub + j * half == rt)
            pt_rim[h, 0:half, c:c + chunk] = hot(sub + rim_j * half == rt)
            pt_rim[h, half:2 * half, c:c + chunk] = hot(sub == rs)
        for c in range(0, edges, chunk):
            part = spread[c:c + chunk]
            y = dot_nt(part, diff)
            r8 = lax.broadcasted_iota(jnp.int32, (chunk, slots), 0) % slots
            l8 = lax.broadcasted_iota(jnp.int32, (chunk, slots), 1)
            y = jnp.where(r8 == l8, y, 0.0).astype(BF)
            b = dot(y, jnp.ones((slots, half), BF))
            atom = ((lax.broadcasted_iota(jnp.int32, (chunk, half), 0) + c) // slots).astype(F32)
            col = lax.broadcasted_iota(jnp.int32, (chunk, half), 1).astype(F32)
            ct = b + atom + half
            cs = jnp.where(b < DEAD / 2, atom, -1.0)
            r0 = h * edges + c
            for pos, j in enumerate(own_js):
                p_own[r0:r0 + chunk, pos * half:(pos + 1) * half] = hot(col + j * half == ct)
            p_rim[r0:r0 + chunk, 0:half] = hot(col + rim_j * half == ct)
            p_rim[r0:r0 + chunk, half:2 * half] = hot(col == cs)

    for i in (2, 3, 4):
        loads[i].wait()
    own_proj[...] = dot(feat[...], wn[...]).astype(BF)
    for h in (0, 1):
        mix[h, half:2 * half] = dot(feat[h * half:(h + 1) * half], ws[...]).astype(BF)

    for i in (5, 6, 7, 8):
        loads[i].wait()

    @pl.loop(0, 2 * edges // chunk)
    def _(i):
        rows = pl.ds(pl.multiple_of(i * chunk, chunk), chunk)
        g = 0.5 * dot(rad[rows], wr[...])
        gate[rows] = g
        had[rows] = dot_nt(cot[rows], wb[...]) * g
        u_own[rows] = dot(p_own[rows], own_proj[...])

    rim_copies = []
    for h in (0, 1):
        halo_copies[h].wait_recv()
        mix[h, 0:half] = dot(halo[h], wn[...]).astype(BF)

        @pl.loop(0, edges // chunk)
        def _(i):
            rows = pl.ds(pl.multiple_of(h * edges + i * chunk, chunk), chunk)
            u = u_own[rows] + dot(p_rim[rows], mix[h])
            p = u * gate[rows]
            t = jnp.tanh(p)
            pt = p * t
            msg[rows] = (p + pt).astype(BF)
            adj[rows] = (had[rows] * ((1.0 + t) * ((1.0 + p) - pt))).astype(BF)

        here = adj.at[pl.ds(h * edges, edges)]
        rim_out[h] = dot(pt_rim[h, 0:half], here[...]).astype(BF)
        copy = pltpu.make_async_remote_copy(
            src_ref=rim_out.at[h], dst_ref=rim_in.at[h],
            send_sem=rim_send.at[h], recv_sem=rim_recv.at[h],
            device_id=((left, right)[h],), device_id_type=MESH)
        copy.start()
        rim_copies.append(copy)

    blk_copies = []
    for c in range(2):
        @pl.loop(0, edges // chunk)
        def _(i):
            rows = pl.ds(pl.multiple_of(c * edges + i * chunk, chunk), chunk)
            blk[rows] = dot(msg[rows], wb[...]).astype(BF)

        part = pl.ds(c * edges, edges)
        copy = pltpu.make_async_copy(blk.at[part], blk_hbm.at[part], blk_sem.at[c])
        copy.start()
        blk_copies.append(copy)

    own_sum[...] = dot(pt_own[...], adj[...])
    for h in (0, 1):
        self_adj[h * half:(h + 1) * half] = dot(
            pt_rim[h, half:2 * half], adj[h * edges:(h + 1) * edges]).astype(BF)
    fg_self[...] = dot_nt(self_adj[...], ws[...])

    fg_copies = []
    for h in (0, 1):
        rim_copies[h].wait_recv()
        rows = pl.ds((1 - h) * half, half)
        total = (own_sum[rows] + rim_in[h].astype(F32)).astype(BF)
        fg[rows] = (fg_self[rows] + dot_nt(total, wn[...])).astype(BF)
        copy = pltpu.make_async_copy(fg.at[rows], fg_hbm.at[rows], fg_sem.at[h])
        copy.start()
        fg_copies.append(copy)

    for copy in blk_copies + fg_copies:
        copy.wait()
    for copy in halo_copies + rim_copies:
        copy.wait_send()


def body(features, radial, neighbours, counts, cotangent, w_self, w_neighbour, w_radial, w_block):
    atoms, width = features.shape
    slots = neighbours.shape[1]
    basis = radial.shape[2]
    out_width = w_block.shape[1]
    half = atoms // 2
    edges = atoms * slots
    n_dev = lax.axis_size("cell")
    any_spec = pl.BlockSpec(memory_space=pl.ANY)
    vm = pltpu.VMEM
    dma = pltpu.SemaphoreType.DMA
    blocks, grad = pl.pallas_call(
        functools.partial(kernel, n_dev, slots, half, 256),
        name="edge_layer",
        out_shape=(
            jax.ShapeDtypeStruct((edges, out_width), BF),
            jax.ShapeDtypeStruct((atoms, width), BF),
        ),
        in_specs=[any_spec] * 9,
        out_specs=(any_spec, any_spec),
        scratch_shapes=[
            vm((atoms, width), BF), vm((edges, basis), BF), vm((slots, atoms), jnp.int32),
            vm((1, atoms), jnp.int32), vm((edges, out_width), BF), vm((width, width), BF),
            vm((width, width), BF), vm((basis, width), BF), vm((width, out_width), BF),
            vm((2, half, width), BF), vm((2, half, width), BF), vm((2, half, width), BF),
            vm((atoms, width), BF), vm((2, 2 * half, width), BF),
            vm((edges, atoms), BF), vm((edges, atoms), BF),
            vm((atoms, edges), BF), vm((2, atoms, edges // 2), BF),
            vm((edges, width), F32), vm((edges, width), F32), vm((edges, width), F32),
            vm((edges, width), BF), vm((edges, width), BF), vm((edges, out_width), BF),
            vm((atoms, width), F32), vm((atoms, width), BF), vm((atoms, width), F32),
            vm((atoms, width), BF),
            dma((9,)), dma((2,)), dma((2,)), dma((2,)), dma((2,)), dma((2,)), dma((2,)),
        ],
        compiler_params=pltpu.CompilerParams(
            collective_id=0, has_side_effects=True, vmem_limit_bytes=56 * 1024 * 1024),
    )(
        features, radial.reshape(edges, basis), neighbours.T, counts.reshape(1, atoms),
        cotangent.reshape(edges, out_width), w_self, w_neighbour, w_radial, w_block,
    )
    return blocks.reshape(atoms, slots, out_width), grad


def solution(mesh):
    in_specs = (
        P("cell", None),
        P("cell", None, None),
        P("cell", None),
        P("cell"),
        P("cell", None, None),
        P(),
        P(),
        P(),
        P(),
    )
    out_specs = (P("cell", None, None), P("cell", None))
    return jax.shard_map(body, mesh=mesh, in_specs=in_specs, out_specs=out_specs, check_vma=False)
```

```python
import functools

import jax
import jax.numpy as jnp
from jax import lax
from jax.experimental import pallas as pl
from jax.experimental.pallas import tpu as pltpu
from jax.sharding import PartitionSpec as P

MESH = pl.DeviceIdType.MESH
BF = jnp.bfloat16
F32 = jnp.float32
DEAD = 1024.0
NT = (((1,), (1,)), ((), ()))


def dot(a, b):
    return jnp.dot(a, b, preferred_element_type=F32)


def dot_nt(a, b):
    return lax.dot_general(a, b, NT, preferred_element_type=F32)


def hot(mask):
    return jnp.where(mask, 1.0, 0.0).astype(BF)


def kernel(
    n_dev, slots, half, chunk,
    feat_hbm, rad_hbm, nbr_hbm, cnt_hbm, cot_hbm, ws_hbm, wn_hbm, wr_hbm, wb_hbm,
    blk, fg,
    feat, rad, nbr, cnt, cot, ws, wn, wr, wb,
    halo, rim_out, rim_in, own_proj, mix, p_own, p_rim, pt_own, pt_rim,
    gate, had, u_own, msg, adj, own_sum, self_adj, fg_self,
    in_sem, halo_send, halo_recv, rim_send, rim_recv,
):
    me = lax.axis_index("cell")
    edges = half * slots

    has = (me > 0, me < n_dev - 1)
    peer = (me - 1, me + 1)

    barrier = pltpu.get_barrier_semaphore()
    for side in (0, 1):
        @pl.when(has[side])
        def _():
            pl.semaphore_signal(barrier, inc=1, device_id=(peer[side],), device_id_type=MESH)

    pairs = [(nbr_hbm, nbr), (cnt_hbm, cnt), (feat_hbm, feat), (wn_hbm, wn), (ws_hbm, ws),
             (rad_hbm, rad), (wr_hbm, wr), (cot_hbm, cot), (wb_hbm, wb)]
    loads = [pltpu.make_async_copy(s, d, in_sem.at[i]) for i, (s, d) in enumerate(pairs)]
    for load in loads:
        load.start()

    pl.semaphore_wait(barrier, has[0].astype(jnp.int32) + has[1].astype(jnp.int32))

    halo_copies = [
        pltpu.make_async_remote_copy(
            src_ref=feat_hbm.at[pl.ds(side * half, half)], dst_ref=halo.at[1 - side],
            send_sem=halo_send.at[side], recv_sem=halo_recv.at[1 - side],
            device_id=(peer[side],), device_id_type=MESH)
        for side in (0, 1)
    ]
    rim_copies = [
        pltpu.make_async_remote_copy(
            src_ref=rim_out.at[side], dst_ref=rim_in.at[1 - side],
            send_sem=rim_send.at[side], recv_sem=rim_recv.at[1 - side],
            device_id=(peer[side],), device_id_type=MESH)
        for side in (0, 1)
    ]
    for side in (0, 1):
        @pl.when(has[side])
        def _():
            halo_copies[side].start()

        @pl.when(jnp.logical_not(has[side]))
        def _():
            halo[side] = jnp.zeros_like(halo[side])
            rim_in[side] = jnp.zeros_like(rim_in[side])

    loads[0].wait()
    loads[1].wait()
    e_row = lax.broadcasted_iota(jnp.int32, (edges, half), 0)
    lane = lax.broadcasted_iota(jnp.int32, (edges, half), 1)
    spread = hot((e_row // slots) == lane)
    slot_of = lax.broadcasted_iota(jnp.int32, (slots, edges), 1)
    atom_lane = (slot_of // slots).astype(F32)
    slot_of = slot_of % slots
    slot_sub = lax.broadcasted_iota(jnp.int32, (slots, edges), 0)
    slot_pick = slot_of == slot_sub
    for h in (0, 1):
        ids = nbr[:, h * half:(h + 1) * half]
        shape = (slots, half)
        base = me * (2 * half) + h * half
        diff = ids - base - lax.broadcasted_iota(jnp.int32, shape, 1)
        live = lax.broadcasted_iota(jnp.int32, shape, 0) < cnt[:, h * half:(h + 1) * half]
        diff = jnp.where(live, diff.astype(F32), DEAD).astype(BF)
        z = jnp.where(slot_pick, dot_nt(diff, spread), 0.0)
        row = jnp.sum(z, axis=0, keepdims=True)
        row_t = row + atom_lane[:1] + half
        row_self = jnp.where(row < DEAD / 2, atom_lane[:1], -1.0)
        own_js = (1, 2) if h == 0 else (0, 1)
        rim_j = 0 if h == 0 else 2
        for c in range(0, edges, chunk):
            sub = lax.broadcasted_iota(jnp.int32, (half, chunk), 0).astype(F32)
            rt = row_t[:, c:c + chunk]
            rs = row_self[:, c:c + chunk]
            for pos, j in enumerate(own_js):
                pt_own[pos * half:(pos + 1) * half, h * edges + c:h * edges + c + chunk] = hot(
                    sub + j * half == rt)
            pt_rim[h, 0:half, c:c + chunk] = hot(sub + rim_j * half == rt)
            pt_rim[h, half:2 * half, c:c + chunk] = hot(sub == rs)
        for c in range(0, edges, chunk):
            part = spread[c:c + chunk]
            y = dot_nt(part, diff)
            r8 = lax.broadcasted_iota(jnp.int32, (chunk, slots), 0) % slots
            l8 = lax.broadcasted_iota(jnp.int32, (chunk, slots), 1)
            y = jnp.where(r8 == l8, y, 0.0).astype(BF)
            b = dot(y, jnp.ones((slots, half), BF))
            atom = ((lax.broadcasted_iota(jnp.int32, (chunk, half), 0) + c) // slots).astype(F32)
            col = lax.broadcasted_iota(jnp.int32, (chunk, half), 1).astype(F32)
            ct = b + atom + half
            cs = jnp.where(b < DEAD / 2, atom, -1.0)
            r0 = h * edges + c
            for pos, j in enumerate(own_js):
                p_own[r0:r0 + chunk, pos * half:(pos + 1) * half] = hot(col + j * half == ct)
            p_rim[r0:r0 + chunk, 0:half] = hot(col + rim_j * half == ct)
            p_rim[r0:r0 + chunk, half:2 * half] = hot(col == cs)

    for i in (2, 3, 4):
        loads[i].wait()
    own_proj[...] = dot(feat[...], wn[...]).astype(BF)
    for h in (0, 1):
        mix[h, half:2 * half] = dot(feat[h * half:(h + 1) * half], ws[...]).astype(BF)

    for i in (5, 6, 7, 8):
        loads[i].wait()

    @pl.loop(0, 2 * edges // chunk, unroll=True)
    def _(i):
        rows = pl.ds(pl.multiple_of(i * chunk, chunk), chunk)
        g = 0.5 * dot(rad[rows], wr[...])
        gate[rows] = g
        had[rows] = dot_nt(cot[rows], wb[...]) * g
        u_own[rows] = dot(p_own[rows], own_proj[...])

    for h in (1, 0):
        @pl.when(has[h])
        def _():
            halo_copies[1 - h].wait_recv()

        mix[h, 0:half] = dot(halo[h], wn[...]).astype(BF)

        @pl.loop(0, edges // chunk, unroll=True)
        def _(i):
            rows = pl.ds(pl.multiple_of(h * edges + i * chunk, chunk), chunk)
            u = u_own[rows] + dot(p_rim[rows], mix[h])
            p = u * gate[rows]
            t = jnp.tanh(p)
            pt = p * t
            msg[rows] = (p + pt).astype(BF)
            adj[rows] = (had[rows] * ((1.0 + t) * ((1.0 + p) - pt))).astype(BF)

        here = adj.at[pl.ds(h * edges, edges)]
        rim_out[h] = dot(pt_rim[h, 0:half], here[...]).astype(BF)

        @pl.when(has[h])
        def _():
            rim_copies[h].start()

    for c in range(2):
        @pl.loop(0, edges // chunk, unroll=True)
        def _(i):
            rows = pl.ds(pl.multiple_of(c * edges + i * chunk, chunk), chunk)
            blk[rows] = dot(msg[rows], wb[...]).astype(BF)

    own_sum[...] = dot(pt_own[...], adj[...])
    for h in (0, 1):
        self_adj[h * half:(h + 1) * half] = dot(
            pt_rim[h, half:2 * half], adj[h * edges:(h + 1) * edges]).astype(BF)
    fg_self[...] = dot_nt(self_adj[...], ws[...])

    for h in (0, 1):
        @pl.when(has[h])
        def _():
            rim_copies[1 - h].wait_recv()

        rows = pl.ds(h * half, half)
        total = (own_sum[rows] + rim_in[h].astype(F32)).astype(BF)
        fg[rows] = (fg_self[rows] + dot_nt(total, wn[...])).astype(BF)

    for side in (0, 1):
        @pl.when(has[side])
        def _():
            halo_copies[side].wait_send()
            rim_copies[side].wait_send()


def store_kernel(blk, fg, blk_hbm, fg_hbm, sem):
    copies = [pltpu.make_async_copy(blk, blk_hbm, sem.at[0]), pltpu.make_async_copy(fg, fg_hbm, sem.at[1])]
    for copy in copies:
        copy.start()
    for copy in copies:
        copy.wait()


def body(features, radial, neighbours, counts, cotangent, w_self, w_neighbour, w_radial, w_block):
    atoms, width = features.shape
    slots = neighbours.shape[1]
    basis = radial.shape[2]
    out_width = w_block.shape[1]
    half = atoms // 2
    edges = atoms * slots
    n_dev = lax.axis_size("cell")
    any_spec = pl.BlockSpec(memory_space=pl.ANY)
    vm = pltpu.VMEM
    dma = pltpu.SemaphoreType.DMA
    blocks, grad = pl.pallas_call(
        functools.partial(kernel, n_dev, slots, half, 256),
        name="edge_layer",
        out_shape=(
            vm((edges, out_width), BF),
            vm((atoms, width), BF),
        ),
        in_specs=[any_spec] * 9,
        out_specs=(pl.BlockSpec(memory_space=vm),) * 2,
        scratch_shapes=[
            vm((atoms, width), BF), vm((edges, basis), BF), vm((slots, atoms), jnp.int32),
            vm((1, atoms), jnp.int32), vm((edges, out_width), BF), vm((width, width), BF),
            vm((width, width), BF), vm((basis, width), BF), vm((width, out_width), BF),
            vm((2, half, width), BF), vm((2, half, width), BF), vm((2, half, width), BF),
            vm((atoms, width), BF), vm((2, 2 * half, width), BF),
            vm((edges, atoms), BF), vm((edges, atoms), BF),
            vm((atoms, edges), BF), vm((2, atoms, edges // 2), BF),
            vm((edges, width), F32), vm((edges, width), F32), vm((edges, width), F32),
            vm((edges, width), BF), vm((edges, width), BF),
            vm((atoms, width), F32), vm((atoms, width), BF), vm((atoms, width), F32),
            dma((9,)), dma((2,)), dma((2,)), dma((2,)), dma((2,)),
        ],
        compiler_params=pltpu.CompilerParams(
            collective_id=0, has_side_effects=True, vmem_limit_bytes=56 * 1024 * 1024),
    )(
        features, radial.reshape(edges, basis), neighbours.T, counts.reshape(1, atoms),
        cotangent.reshape(edges, out_width), w_self, w_neighbour, w_radial, w_block,
    )
    blocks, grad = pl.pallas_call(
        store_kernel,
        name="store",
        out_shape=(
            jax.ShapeDtypeStruct((edges, out_width), BF),
            jax.ShapeDtypeStruct((atoms, width), BF),
        ),
        in_specs=[pl.BlockSpec(memory_space=vm)] * 2,
        out_specs=(any_spec, any_spec),
        scratch_shapes=[dma((2,))],
    )(pltpu.with_memory_space_constraint(blocks, pltpu.VMEM), pltpu.with_memory_space_constraint(grad, pltpu.VMEM))
    return blocks.reshape(atoms, slots, out_width), grad


def solution(mesh):
    in_specs = (
        P("cell", None),
        P("cell", None, None),
        P("cell", None),
        P("cell"),
        P("cell", None, None),
        P(),
        P(),
        P(),
        P(),
    )
    out_specs = (P("cell", None, None), P("cell", None))
    return jax.shard_map(body, mesh=mesh, in_specs=in_specs, out_specs=out_specs, check_vma=False)
```

```python
import functools

import jax
import jax.numpy as jnp
from jax import lax
from jax.experimental import pallas as pl
from jax.experimental.pallas import tpu as pltpu
from jax.sharding import PartitionSpec as P

MESH = pl.DeviceIdType.MESH
BF = jnp.bfloat16
F32 = jnp.float32
DEAD = 1024.0
COLS = 2
ROUND = 128
RELAY = 14
NT = (((1,), (1,)), ((), ()))


def dot(a, b):
    return jnp.dot(a, b, preferred_element_type=F32)


def dot_nt(a, b):
    return lax.dot_general(a, b, NT, preferred_element_type=F32)


def hot(mask):
    return jnp.where(mask, 1.0, 0.0).astype(BF)


def kernel(
    n_dev, slots, half, chunk,
    feat_hbm, rad_hbm, nbr_hbm, cnt_hbm, cot_hbm, ws_hbm, wn_hbm, wr_hbm, wb_hbm,
    blk, fg,
    feat, rad, nbr, cnt, cot, ws, wn, wr, wb,
    halo, passed, rim_out, rim_in, proj, p_own, p_rim, pt_own, pt_rim, pt_self,
    gate, had, u_own, msg, adj, own_sum, fg_self,
    in_sem, halo_send, halo_recv, pass_send, pass_recv, rim_send, rim_recv,
):
    me = lax.axis_index("cell")
    has = (me > 0, me < n_dev - 1)
    peer = (me - 1, me + 1)
    spot = lax.rem(me, ROUND)
    far_low = jnp.logical_and(spot == ROUND - 1, has[1])
    far_high = jnp.logical_and(spot == 0, has[0])
    relay = jnp.logical_and(spot == RELAY, me + ROUND < n_dev)
    greet = (me - 1, jnp.where(far_low, me - (ROUND - 1 - RELAY), me + 1))
    edges = half * slots
    width = feat.shape[1]
    part = width // COLS

    barrier = pltpu.get_barrier_semaphore()
    for side in (0, 1):
        @pl.when(has[side])
        def _():
            pl.semaphore_signal(barrier, inc=1, device_id=(greet[side],), device_id_type=MESH)

    @pl.when(relay)
    def _():
        pl.semaphore_signal(
            barrier, inc=1, device_id=(me + ROUND - RELAY,), device_id_type=MESH)

    pairs = [(feat_hbm, feat), (wn_hbm, wn), (nbr_hbm, nbr), (cnt_hbm, cnt), (ws_hbm, ws),
             (rad_hbm, rad), (wr_hbm, wr), (cot_hbm, cot), (wb_hbm, wb)]
    loads = [pltpu.make_async_copy(s, d, in_sem.at[i]) for i, (s, d) in enumerate(pairs)]
    for load in loads:
        load.start()

    loads[0].wait()
    loads[1].wait()
    own = dot(feat[...], wn[...]).astype(BF)
    for h in (0, 1):
        proj[h, 0:2 * half] = own

    halo_copies = [[
        pltpu.make_async_remote_copy(
            src_ref=proj.at[0, pl.ds(side * half, half), pl.ds(c * part, part)],
            dst_ref=halo.at[1 - side, c],
            send_sem=halo_send.at[side, c], recv_sem=halo_recv.at[1 - side, c],
            device_id=(peer[side],), device_id_type=MESH)
        for c in range(COLS)] for side in (0, 1)]
    rim_copies = [[
        pltpu.make_async_remote_copy(
            src_ref=rim_out.at[side, c], dst_ref=rim_in.at[1 - side, c],
            send_sem=rim_send.at[side, c], recv_sem=rim_recv.at[1 - side, c],
            device_id=(peer[side],), device_id_type=MESH)
        for c in range(COLS)] for side in (0, 1)]

    pass_in = [
        pltpu.make_async_remote_copy(
            src_ref=proj.at[0, pl.ds(0, half), pl.ds(c * part, part)], dst_ref=passed.at[c],
            send_sem=halo_send.at[0, c], recv_sem=pass_recv.at[c],
            device_id=(me - (ROUND - RELAY),), device_id_type=MESH)
        for c in range(COLS)]
    pass_on = [
        pltpu.make_async_remote_copy(
            src_ref=passed.at[c], dst_ref=halo.at[1, c],
            send_sem=pass_send.at[c], recv_sem=halo_recv.at[1, c],
            device_id=(me + (ROUND - 1 - RELAY),), device_id_type=MESH)
        for c in range(COLS)]

    def meet():
        count = has[0].astype(jnp.int32) + has[1].astype(jnp.int32) + relay.astype(jnp.int32)
        pl.semaphore_wait(barrier, count)

        @pl.when(far_high)
        def _():
            for copy in pass_in:
                copy.start()

        @pl.when(jnp.logical_and(has[0], jnp.logical_not(far_high)))
        def _():
            for copy in halo_copies[0]:
                copy.start()

        @pl.when(has[1])
        def _():
            for copy in halo_copies[1]:
                copy.start()

    @pl.when(jnp.logical_not(relay))
    def _():
        meet()

    for side in (0, 1):
        @pl.when(jnp.logical_not(has[side]))
        def _():
            halo[side] = jnp.zeros_like(halo[side])
            rim_in[side] = jnp.zeros_like(rim_in[side])

    loads[2].wait()
    loads[3].wait()
    e_row = lax.broadcasted_iota(jnp.int32, (edges, half), 0)
    lane = lax.broadcasted_iota(jnp.int32, (edges, half), 1)
    spread = hot((e_row // slots) == lane)
    slot_of = lax.broadcasted_iota(jnp.int32, (slots, edges), 1)
    atom_lane = (slot_of // slots).astype(F32)
    slot_of = slot_of % slots
    slot_sub = lax.broadcasted_iota(jnp.int32, (slots, edges), 0)
    slot_pick = slot_of == slot_sub
    for h in (1, 0):
        ids = nbr[:, h * half:(h + 1) * half]
        shape = (slots, half)
        base = me * (2 * half) + h * half
        diff = ids - base - lax.broadcasted_iota(jnp.int32, shape, 1)
        live = lax.broadcasted_iota(jnp.int32, shape, 0) < cnt[:, h * half:(h + 1) * half]
        diff = jnp.where(live, diff.astype(F32), DEAD).astype(BF)
        z = jnp.where(slot_pick, dot_nt(diff, spread), 0.0)
        row = jnp.sum(z, axis=0, keepdims=True)
        row_t = row + atom_lane[:1] + half
        row_self = jnp.where(row < DEAD / 2, atom_lane[:1], -1.0)
        own_js = (1, 2) if h == 0 else (0, 1)
        rim_j = 0 if h == 0 else 2
        for c in range(0, edges, chunk):
            sub = lax.broadcasted_iota(jnp.int32, (half, chunk), 0).astype(F32)
            rt = row_t[:, c:c + chunk]
            rs = row_self[:, c:c + chunk]
            for pos, j in enumerate(own_js):
                pt_own[pos * half:(pos + 1) * half, h * edges + c:h * edges + c + chunk] = hot(
                    sub + j * half == rt)
            pt_rim[h, :, c:c + chunk] = hot(sub + rim_j * half == rt)
            pt_self[h, :, c:c + chunk] = hot(sub == rs)
        for c in range(0, edges, chunk):
            y = dot_nt(spread[c:c + chunk], diff)
            r8 = lax.broadcasted_iota(jnp.int32, (chunk, slots), 0) % slots
            l8 = lax.broadcasted_iota(jnp.int32, (chunk, slots), 1)
            y = jnp.where(r8 == l8, y, 0.0).astype(BF)
            b = dot(y, jnp.ones((slots, half), BF))
            atom = ((lax.broadcasted_iota(jnp.int32, (chunk, half), 0) + c) // slots).astype(F32)
            col = lax.broadcasted_iota(jnp.int32, (chunk, half), 1).astype(F32)
            ct = b + atom + half
            cs = jnp.where(b < DEAD / 2, atom, -1.0)
            rows = slice(h * edges + c, h * edges + c + chunk)
            for pos, j in enumerate(own_js):
                p_own[rows, pos * half:(pos + 1) * half] = hot(col + j * half == ct)
            p_own[rows, 2 * half:3 * half] = hot(col == cs)
            p_rim[rows] = hot(col + rim_j * half == ct)

    loads[4].wait()
    for h in (0, 1):
        proj[h, 2 * half:3 * half] = dot(feat[h * half:(h + 1) * half], ws[...]).astype(BF)

    for i in (5, 6, 7, 8):
        loads[i].wait()

    for h in (1, 0):
        @pl.loop(0, edges // chunk, unroll=True)
        def _(i):
            rows = pl.ds(pl.multiple_of(h * edges + i * chunk, chunk), chunk)
            g = 0.5 * dot(rad[rows], wr[...])
            gate[rows] = g
            had[rows] = dot_nt(cot[rows], wb[...]) * g
            u_own[rows] = dot(p_own[rows], proj[h])

    @pl.when(relay)
    def _():
        meet()
        for c in range(COLS):
            pass_in[c].wait_recv()
            pass_on[c].start()

    for h in (1, 0):
        for c in range(COLS):
            cols = slice(c * part, (c + 1) * part)

            @pl.when(has[h])
            def _():
                halo_copies[1 - h][c].wait_recv()

            for r in range(0, edges, chunk):
                rows = slice(h * edges + r, h * edges + r + chunk)
                u = u_own[rows, cols] + dot(p_rim[rows], halo[h, c])
                p = u * gate[rows, cols]
                t = jnp.tanh(p)
                pt = p * t
                msg[rows, cols] = (p + pt).astype(BF)
                adj[rows, cols] = (had[rows, cols] * ((1.0 + t) * ((1.0 + p) - pt))).astype(BF)

            rim_out[h, c] = dot(pt_rim[h], adj[h * edges:(h + 1) * edges, cols]).astype(BF)

            @pl.when(has[h])
            def _():
                rim_copies[h][c].start()

        for r in range(0, edges, chunk):
            rows = slice(h * edges + r, h * edges + r + chunk)
            blk[rows] = dot(msg[rows], wb[...]).astype(BF)

        mine = slice(h * edges, (h + 1) * edges)
        own_part = dot(pt_own[:, mine], adj[mine])
        own_sum[...] = own_part if h == 1 else own_sum[...] + own_part
        self_adj = dot(pt_self[h], adj[mine]).astype(BF)
        fg_self[h * half:(h + 1) * half] = dot_nt(self_adj, ws[...])

    for h in (1, 0):
        rows = slice(h * half, (h + 1) * half)
        total = fg_self[rows]
        for c in range(COLS):
            cols = slice(c * part, (c + 1) * part)

            @pl.when(has[h])
            def _():
                rim_copies[1 - h][c].wait_recv()

            nbr_adj = (own_sum[rows, cols] + rim_in[h, c].astype(F32)).astype(BF)
            total = total + dot_nt(nbr_adj, wn[:, cols])
        fg[rows] = total.astype(BF)

    for side in (0, 1):
        @pl.when(has[side])
        def _():
            for copy in halo_copies[side] + rim_copies[side]:
                copy.wait_send()

    @pl.when(relay)
    def _():
        for copy in pass_on:
            copy.wait_send()


def store_kernel(blk, fg, blk_hbm, fg_hbm, sem):
    copies = [
        pltpu.make_async_copy(blk, blk_hbm, sem.at[0]),
        pltpu.make_async_copy(fg, fg_hbm, sem.at[1]),
    ]
    for copy in copies:
        copy.start()
    for copy in copies:
        copy.wait()


def body(features, radial, neighbours, counts, cotangent, w_self, w_neighbour, w_radial, w_block):
    atoms, width = features.shape
    slots = neighbours.shape[1]
    basis = radial.shape[2]
    out_width = w_block.shape[1]
    half = atoms // 2
    edges = atoms * slots
    part = width // COLS
    n_dev = lax.axis_size("cell")
    any_spec = pl.BlockSpec(memory_space=pl.ANY)
    vm = pltpu.VMEM
    dma = pltpu.SemaphoreType.DMA
    vm_spec = pl.BlockSpec(memory_space=vm)
    blocks, grad = pl.pallas_call(
        functools.partial(kernel, n_dev, slots, half, 256),
        name="edge_layer",
        out_shape=(vm((edges, out_width), BF), vm((atoms, width), BF)),
        in_specs=[any_spec] * 9,
        out_specs=(vm_spec,) * 2,
        scratch_shapes=[
            vm((atoms, width), BF), vm((edges, basis), BF), vm((slots, atoms), jnp.int32),
            vm((1, atoms), jnp.int32), vm((edges, out_width), BF), vm((width, width), BF),
            vm((width, width), BF), vm((basis, width), BF), vm((width, out_width), BF),
            vm((2, COLS, half, part), BF), vm((COLS, half, part), BF),
            vm((2, COLS, half, part), BF), vm((2, COLS, half, part), BF),
            vm((2, 3 * half, width), BF),
            vm((edges, 3 * half), BF), vm((edges, half), BF),
            vm((atoms, edges), BF), vm((2, half, edges // 2), BF), vm((2, half, edges // 2), BF),
            vm((edges, width), F32), vm((edges, width), F32), vm((edges, width), F32),
            vm((edges, width), BF), vm((edges, width), BF),
            vm((atoms, width), F32), vm((atoms, width), F32),
            dma((9,)), dma((2, COLS)), dma((2, COLS)), dma((COLS,)), dma((COLS,)),
            dma((2, COLS)), dma((2, COLS)),
        ],
        compiler_params=pltpu.CompilerParams(
            collective_id=0, has_side_effects=True, vmem_limit_bytes=56 * 1024 * 1024),
    )(
        features, radial.reshape(edges, basis), neighbours.T, counts.reshape(1, atoms),
        cotangent.reshape(edges, out_width), w_self, w_neighbour, w_radial, w_block,
    )
    blocks, grad = pl.pallas_call(
        store_kernel,
        name="store",
        out_shape=(
            jax.ShapeDtypeStruct((edges, out_width), BF),
            jax.ShapeDtypeStruct((atoms, width), BF),
        ),
        in_specs=[vm_spec] * 2,
        out_specs=(any_spec, any_spec),
        scratch_shapes=[dma((2,))],
    )(
        pltpu.with_memory_space_constraint(blocks, vm),
        pltpu.with_memory_space_constraint(grad, vm),
    )
    return blocks.reshape(atoms, slots, out_width), grad


def solution(mesh):
    in_specs = (
        P("cell", None),
        P("cell", None, None),
        P("cell", None),
        P("cell"),
        P("cell", None, None),
        P(),
        P(),
        P(),
        P(),
    )
    out_specs = (P("cell", None, None), P("cell", None))
    return jax.shard_map(body, mesh=mesh, in_specs=in_specs, out_specs=out_specs, check_vma=False)
```

```python
import functools

import jax
import jax.numpy as jnp
from jax import lax
from jax.experimental import pallas as pl
from jax.experimental.pallas import tpu as pltpu
from jax.sharding import PartitionSpec as P

MESH = pl.DeviceIdType.MESH
BF = jnp.bfloat16
F32 = jnp.float32
DEAD = 1024.0
PARTS = ((0, 4), (4, 4))
COLS = len(PARTS)
ROUND = 128
RELAY = 14
NT = (((1,), (1,)), ((), ()))


def dot(a, b):
    return jnp.dot(a, b, preferred_element_type=F32)


def dot_nt(a, b):
    return lax.dot_general(a, b, NT, preferred_element_type=F32)


def hot(mask):
    return jnp.where(mask, 1.0, 0.0).astype(BF)


def kernel(
    n_dev, slots, half, chunk,
    feat_hbm, rad_hbm, nbr_hbm, cnt_hbm, cot_hbm, ws_hbm, wn_hbm, wr_hbm, wb_hbm,
    blk, fg_self, nbr_adj, wn,
    feat, rad, nbr, cnt, cot, ws, wr, wb,
    halo, passed, rim_out, rim_in, proj, p_own, p_rim, pt_own, pt_rim, pt_self,
    gate, had, u_own, msg, adj, own_sum,
    in_sem, halo_send, halo_recv, pass_send, pass_recv, rim_send, rim_recv,
):
    me = lax.axis_index("cell")
    has = (me > 0, me < n_dev - 1)
    peer = (me - 1, me + 1)
    spot = lax.rem(me, ROUND)
    far_low = jnp.logical_and(spot == ROUND - 1, has[1])
    far_high = jnp.logical_and(spot == 0, has[0])
    relay = jnp.logical_and(spot == RELAY, me + ROUND < n_dev)
    late = jnp.logical_or(relay, me == 1)
    greet = (me - 1, jnp.where(far_low, me - (ROUND - 1 - RELAY), me + 1))
    edges = half * slots
    width = feat.shape[1]
    spans = [(a * width // 8, n * width // 8) for a, n in PARTS]

    barrier = pltpu.get_barrier_semaphore()
    for side in (1, 0):
        @pl.when(has[side])
        def _():
            pl.semaphore_signal(barrier, inc=1, device_id=(greet[side],), device_id_type=MESH)

    @pl.when(relay)
    def _():
        pl.semaphore_signal(
            barrier, inc=1, device_id=(me + ROUND - RELAY,), device_id_type=MESH)

    pairs = [(feat_hbm, feat), (wn_hbm, wn), (nbr_hbm, nbr), (cnt_hbm, cnt), (ws_hbm, ws),
             (rad_hbm, rad), (wr_hbm, wr), (cot_hbm, cot), (wb_hbm, wb)]
    loads = [pltpu.make_async_copy(s, d, in_sem.at[i]) for i, (s, d) in enumerate(pairs)]
    for load in loads:
        load.start()

    halo_copies = [[
        pltpu.make_async_remote_copy(
            src_ref=proj.at[0, pl.ds(side * half, half), pl.ds(*spans[c])],
            dst_ref=halo.at[1 - side, :, pl.ds(*spans[c])],
            send_sem=halo_send.at[side, c], recv_sem=halo_recv.at[1 - side, c],
            device_id=(peer[side],), device_id_type=MESH)
        for c in range(COLS)] for side in (0, 1)]
    rim_copies = [[
        pltpu.make_async_remote_copy(
            src_ref=rim_out.at[side, :, pl.ds(*spans[c])],
            dst_ref=rim_in.at[1 - side, :, pl.ds(*spans[c])],
            send_sem=rim_send.at[side, c], recv_sem=rim_recv.at[1 - side, c],
            device_id=(peer[side],), device_id_type=MESH)
        for c in range(COLS)] for side in (0, 1)]

    pass_in = [
        pltpu.make_async_remote_copy(
            src_ref=proj.at[0, pl.ds(0, half), pl.ds(*spans[c])], dst_ref=passed.at[:, pl.ds(*spans[c])],
            send_sem=halo_send.at[0, c], recv_sem=pass_recv.at[c],
            device_id=(me - (ROUND - RELAY),), device_id_type=MESH)
        for c in range(COLS)]
    pass_on = [
        pltpu.make_async_remote_copy(
            src_ref=passed.at[:, pl.ds(*spans[c])], dst_ref=halo.at[1, :, pl.ds(*spans[c])],
            send_sem=pass_send.at[c], recv_sem=halo_recv.at[1, c],
            device_id=(me + (ROUND - 1 - RELAY),), device_id_type=MESH)
        for c in range(COLS)]

    def meet():
        count = has[0].astype(jnp.int32) + has[1].astype(jnp.int32) + relay.astype(jnp.int32)
        pl.semaphore_wait(barrier, count)

        @pl.when(relay)
        def _():
            for c in range(COLS):
                pass_in[c].wait_recv()
                pass_on[c].start()

        @pl.when(far_high)
        def _():
            for copy in pass_in:
                copy.start()

        @pl.when(jnp.logical_and(has[0], jnp.logical_not(far_high)))
        def _():
            for copy in halo_copies[0]:
                copy.start()

        @pl.when(has[1])
        def _():
            for copy in halo_copies[1]:
                copy.start()

    loads[2].wait()
    loads[3].wait()
    e_row = lax.broadcasted_iota(jnp.int32, (edges, half), 0)
    lane = lax.broadcasted_iota(jnp.int32, (edges, half), 1)
    spread = hot((e_row // slots) == lane)
    slot_of = lax.broadcasted_iota(jnp.int32, (slots, edges), 1)
    atom_lane = (slot_of // slots).astype(F32)
    slot_of = slot_of % slots
    slot_sub = lax.broadcasted_iota(jnp.int32, (slots, edges), 0)
    slot_pick = slot_of == slot_sub
    def select(h):
        ids = nbr[:, h * half:(h + 1) * half]
        shape = (slots, half)
        base = me * (2 * half) + h * half
        diff = ids - base - lax.broadcasted_iota(jnp.int32, shape, 1)
        live = lax.broadcasted_iota(jnp.int32, shape, 0) < cnt[:, h * half:(h + 1) * half]
        diff = jnp.where(live, diff.astype(F32), DEAD).astype(BF)
        z = jnp.where(slot_pick, dot_nt(diff, spread), 0.0)
        row = jnp.sum(z, axis=0, keepdims=True)
        row_t = row + atom_lane[:1] + half
        row_self = jnp.where(row < DEAD / 2, atom_lane[:1], -1.0)
        own_js = (1, 2) if h == 0 else (0, 1)
        rim_j = 0 if h == 0 else 2
        for c in range(0, edges, chunk):
            sub = lax.broadcasted_iota(jnp.int32, (half, chunk), 0).astype(F32)
            rt = row_t[:, c:c + chunk]
            rs = row_self[:, c:c + chunk]
            for pos, j in enumerate(own_js):
                pt_own[pos * half:(pos + 1) * half, h * edges + c:h * edges + c + chunk] = hot(
                    sub + j * half == rt)
            pt_rim[h, :, c:c + chunk] = hot(sub + rim_j * half == rt)
            pt_self[h, :, c:c + chunk] = hot(sub == rs)
        for c in range(0, edges, chunk):
            y = dot_nt(spread[c:c + chunk], diff)
            r8 = lax.broadcasted_iota(jnp.int32, (chunk, slots), 0) % slots
            l8 = lax.broadcasted_iota(jnp.int32, (chunk, slots), 1)
            y = jnp.where(r8 == l8, y, 0.0).astype(BF)
            b = dot(y, jnp.ones((slots, half), BF))
            atom = ((lax.broadcasted_iota(jnp.int32, (chunk, half), 0) + c) // slots).astype(F32)
            col = lax.broadcasted_iota(jnp.int32, (chunk, half), 1).astype(F32)
            ct = b + atom + half
            cs = jnp.where(b < DEAD / 2, atom, -1.0)
            rows = slice(h * edges + c, h * edges + c + chunk)
            for pos, j in enumerate(own_js):
                p_own[rows, pos * half:(pos + 1) * half] = hot(col + j * half == ct)
            p_own[rows, 2 * half:3 * half] = hot(col == cs)
            p_rim[rows] = hot(col + rim_j * half == ct)

    def prepare(h):
        if h == 1:
            loads[4].wait()
        proj[h, 2 * half:3 * half] = dot(feat[h * half:(h + 1) * half], ws[...]).astype(BF)
        if h == 1:
            for i in (5, 6, 7, 8):
                loads[i].wait()

        @pl.loop(0, edges // chunk, unroll=True)
        def _(i):
            rows = pl.ds(pl.multiple_of(h * edges + i * chunk, chunk), chunk)
            g = 0.5 * dot(rad[rows], wr[...])
            gate[rows] = g
            had[rows] = dot_nt(cot[rows], wb[...]) * g
            u_own[rows] = dot(p_own[rows], proj[h])

    def stages(h):
        for c in range(COLS):
            cols = slice(spans[c][0], sum(spans[c]))

            @pl.when(has[h])
            def _():
                halo_copies[1 - h][c].wait_recv()

            for r in range(0, edges, chunk):
                rows = slice(h * edges + r, h * edges + r + chunk)
                u = u_own[rows, cols] + dot(p_rim[rows], halo[h, :, cols])
                p = u * gate[rows, cols]
                t = jnp.tanh(p)
                pt = p * t
                msg[rows, cols] = (p + pt).astype(BF)
                adj[rows, cols] = (had[rows, cols] * ((1.0 + t) * ((1.0 + p) - pt))).astype(BF)

            rim_out[h, :, cols] = dot(pt_rim[h], adj[h * edges:(h + 1) * edges, cols]).astype(BF)

            @pl.when(has[h])
            def _():
                rim_copies[h][c].start()

    def rest(h, first):
        for r in range(0, edges, chunk):
            rows = slice(h * edges + r, h * edges + r + chunk)
            blk[rows] = dot(msg[rows], wb[...]).astype(BF)

        mine = slice(h * edges, (h + 1) * edges)
        own_part = dot(pt_own[:, mine], adj[mine])
        own_sum[...] = own_part if first else own_sum[...] + own_part
        self_adj = dot(pt_self[h], adj[mine]).astype(BF)
        fg_self[h * half:(h + 1) * half] = dot_nt(self_adj, ws[...])

    select(1)
    loads[0].wait()
    loads[1].wait()
    own = dot(feat[...], wn[...]).astype(BF)
    for h in (0, 1):
        proj[h, 0:2 * half] = own

    @pl.when(jnp.logical_not(late))
    def _():
        meet()

    for side in (0, 1):
        @pl.when(jnp.logical_not(has[side]))
        def _():
            halo[side] = jnp.zeros_like(halo[side])
            rim_in[side] = jnp.zeros_like(rim_in[side])

    prepare(1)
    @pl.when(late)
    def _():
        meet()

    stages(1)
    select(0)
    prepare(0)
    stages(0)
    rest(1, True)
    rest(0, False)

    for h in (1, 0):
        rows = slice(h * half, (h + 1) * half)
        for c in range(COLS):
            cols = slice(spans[c][0], sum(spans[c]))

            @pl.when(has[h])
            def _():
                rim_copies[1 - h][c].wait_recv()

            nbr_adj[rows, cols] = (own_sum[rows, cols] + rim_in[h, :, cols].astype(F32)).astype(BF)

    for side in (0, 1):
        @pl.when(has[side])
        def _():
            for copy in halo_copies[side] + rim_copies[side]:
                copy.wait_send()

    @pl.when(relay)
    def _():
        for copy in pass_on:
            copy.wait_send()


def finish_kernel(blk, fg_self, nbr_adj, wn, blk_hbm, fg_hbm, fg, sem):
    copies = [pltpu.make_async_copy(blk, blk_hbm, sem.at[2])]
    copies[0].start()
    half = fg.shape[0] // 2
    for h in (0, 1):
        rows = pl.ds(h * half, half)
        fg[rows] = (fg_self[rows] + dot_nt(nbr_adj[rows], wn[...])).astype(BF)
        copies.append(pltpu.make_async_copy(fg.at[rows], fg_hbm.at[rows], sem.at[h]))
        copies[-1].start()
    for copy in copies:
        copy.wait()


def body(features, radial, neighbours, counts, cotangent, w_self, w_neighbour, w_radial, w_block):
    atoms, width = features.shape
    slots = neighbours.shape[1]
    basis = radial.shape[2]
    out_width = w_block.shape[1]
    half = atoms // 2
    edges = atoms * slots
    n_dev = lax.axis_size("cell")
    any_spec = pl.BlockSpec(memory_space=pl.ANY)
    vm = pltpu.VMEM
    dma = pltpu.SemaphoreType.DMA
    vm_spec = pl.BlockSpec(memory_space=vm)
    parts = pl.pallas_call(
        functools.partial(kernel, n_dev, slots, half, 256),
        name="edge_layer",
        out_shape=(
            vm((edges, out_width), BF), vm((atoms, width), F32),
            vm((atoms, width), BF), vm((width, width), BF),
        ),
        in_specs=[any_spec] * 9,
        out_specs=(vm_spec,) * 4,
        scratch_shapes=[
            vm((atoms, width), BF), vm((edges, basis), BF), vm((slots, atoms), jnp.int32),
            vm((1, atoms), jnp.int32), vm((edges, out_width), BF), vm((width, width), BF),
            vm((basis, width), BF), vm((width, out_width), BF),
            vm((2, half, width), BF), vm((half, width), BF),
            vm((2, half, width), BF), vm((2, half, width), BF),
            vm((2, 3 * half, width), BF),
            vm((edges, 3 * half), BF), vm((edges, half), BF),
            vm((atoms, edges), BF), vm((2, half, edges // 2), BF), vm((2, half, edges // 2), BF),
            vm((edges, width), F32), vm((edges, width), F32), vm((edges, width), F32),
            vm((edges, width), BF), vm((edges, width), BF),
            vm((atoms, width), F32),
            dma((9,)), dma((2, COLS)), dma((2, COLS)), dma((COLS,)), dma((COLS,)),
            dma((2, COLS)), dma((2, COLS)),
        ],
        compiler_params=pltpu.CompilerParams(
            collective_id=0, has_side_effects=True, vmem_limit_bytes=56 * 1024 * 1024),
    )(
        features, radial.reshape(edges, basis), neighbours.T, counts.reshape(1, atoms),
        cotangent.reshape(edges, out_width), w_self, w_neighbour, w_radial, w_block,
    )
    blocks, grad = pl.pallas_call(
        finish_kernel,
        name="finish",
        out_shape=(
            jax.ShapeDtypeStruct((edges, out_width), BF),
            jax.ShapeDtypeStruct((atoms, width), BF),
        ),
        in_specs=[vm_spec] * 4,
        out_specs=(any_spec, any_spec),
        scratch_shapes=[vm((atoms, width), BF), dma((3,))],
    )(*[pltpu.with_memory_space_constraint(array, vm) for array in parts])
    return blocks.reshape(atoms, slots, out_width), grad


def solution(mesh):
    in_specs = (
        P("cell", None),
        P("cell", None, None),
        P("cell", None),
        P("cell"),
        P("cell", None, None),
        P(),
        P(),
        P(),
        P(),
    )
    out_specs = (P("cell", None, None), P("cell", None))
    return jax.shard_map(body, mesh=mesh, in_specs=in_specs, out_specs=out_specs, check_vma=False)
```

```python
import functools

import jax
import jax.numpy as jnp
from jax import lax
from jax.experimental import pallas as pl
from jax.experimental.pallas import tpu as pltpu
from jax.sharding import PartitionSpec as P

MESH = pl.DeviceIdType.MESH
BF = jnp.bfloat16
F32 = jnp.float32
DEAD = 1024.0
PARTS = ((0, 4), (4, 4))
COLS = len(PARTS)
ROUND = 128
RELAY = 14
NT = (((1,), (1,)), ((), ()))


def dot(a, b):
    return jnp.dot(a, b, preferred_element_type=F32)


def dot_nt(a, b):
    return lax.dot_general(a, b, NT, preferred_element_type=F32)


def hot(mask):
    return jnp.where(mask, 1.0, 0.0).astype(BF)


def kernel(
    n_dev, slots, half, chunk,
    feat_hbm, rad_hbm, nbr_hbm, cnt_hbm, cot_hbm, ws_hbm, wn_hbm, wr_hbm, wb_hbm,
    blk, fg_high, fg_low, nbr_adj, wn,
    feat, rad, nbr, cnt, cot, ws, wr, wb,
    halo, passed, rim_out, rim_in, proj, p_own, p_rim, pt_own, pt_rim, pt_self,
    gate, had, u_own, msg, adj, own_sum, fg_part,
    in_sem, halo_send, halo_recv, pass_send, pass_recv, rim_send, rim_recv,
):
    me = lax.axis_index("cell")
    has = (me > 0, me < n_dev - 1)
    peer = (me - 1, me + 1)
    spot = lax.rem(me, ROUND)
    far_low = jnp.logical_and(spot == ROUND - 1, has[1])
    far_high = jnp.logical_and(spot == 0, has[0])
    relay = jnp.logical_and(spot == RELAY, me + ROUND < n_dev)
    late = jnp.logical_or(relay, me == 1)
    greet = (me - 1, jnp.where(far_low, me - (ROUND - 1 - RELAY), me + 1))
    edges = half * slots
    width = feat.shape[1]
    spans = [(a * width // 8, n * width // 8) for a, n in PARTS]

    barrier = pltpu.get_barrier_semaphore()
    for side in (1, 0):
        @pl.when(has[side])
        def _():
            pl.semaphore_signal(barrier, inc=1, device_id=(greet[side],), device_id_type=MESH)

    @pl.when(relay)
    def _():
        pl.semaphore_signal(
            barrier, inc=1, device_id=(me + ROUND - RELAY,), device_id_type=MESH)

    pairs = [(feat_hbm, feat), (wn_hbm, wn), (nbr_hbm, nbr), (cnt_hbm, cnt), (ws_hbm, ws),
             (rad_hbm, rad), (wr_hbm, wr), (cot_hbm, cot), (wb_hbm, wb)]
    loads = [pltpu.make_async_copy(s, d, in_sem.at[i]) for i, (s, d) in enumerate(pairs)]
    for load in loads:
        load.start()

    halo_copies = [[
        pltpu.make_async_remote_copy(
            src_ref=proj.at[0, pl.ds(side * half, half), pl.ds(*spans[c])],
            dst_ref=halo.at[1 - side, :, pl.ds(*spans[c])],
            send_sem=halo_send.at[side, c], recv_sem=halo_recv.at[1 - side, c],
            device_id=(peer[side],), device_id_type=MESH)
        for c in range(COLS)] for side in (0, 1)]
    rim_copies = [[
        pltpu.make_async_remote_copy(
            src_ref=rim_out.at[side, :, pl.ds(*spans[c])],
            dst_ref=rim_in.at[1 - side, :, pl.ds(*spans[c])],
            send_sem=rim_send.at[side, c], recv_sem=rim_recv.at[1 - side, c],
            device_id=(peer[side],), device_id_type=MESH)
        for c in range(COLS)] for side in (0, 1)]

    pass_in = [
        pltpu.make_async_remote_copy(
            src_ref=proj.at[0, pl.ds(0, half), pl.ds(*spans[c])], dst_ref=passed.at[:, pl.ds(*spans[c])],
            send_sem=halo_send.at[0, c], recv_sem=pass_recv.at[c],
            device_id=(me - (ROUND - RELAY),), device_id_type=MESH)
        for c in range(COLS)]
    pass_on = [
        pltpu.make_async_remote_copy(
            src_ref=passed.at[:, pl.ds(*spans[c])], dst_ref=halo.at[1, :, pl.ds(*spans[c])],
            send_sem=pass_send.at[c], recv_sem=halo_recv.at[1, c],
            device_id=(me + (ROUND - 1 - RELAY),), device_id_type=MESH)
        for c in range(COLS)]

    def meet():
        count = has[0].astype(jnp.int32) + has[1].astype(jnp.int32) + relay.astype(jnp.int32)
        pl.semaphore_wait(barrier, count)

        @pl.when(relay)
        def _():
            for c in range(COLS):
                pass_in[c].wait_recv()
                pass_on[c].start()

        @pl.when(far_high)
        def _():
            for copy in pass_in:
                copy.start()

        @pl.when(jnp.logical_and(has[0], jnp.logical_not(far_high)))
        def _():
            for copy in halo_copies[0]:
                copy.start()

        @pl.when(has[1])
        def _():
            for copy in halo_copies[1]:
                copy.start()

    loads[2].wait()
    loads[3].wait()
    e_row = lax.broadcasted_iota(jnp.int32, (edges, half), 0)
    lane = lax.broadcasted_iota(jnp.int32, (edges, half), 1)
    spread = hot((e_row // slots) == lane)
    slot_of = lax.broadcasted_iota(jnp.int32, (slots, edges), 1)
    atom_lane = (slot_of // slots).astype(F32)
    slot_of = slot_of % slots
    slot_sub = lax.broadcasted_iota(jnp.int32, (slots, edges), 0)
    slot_pick = slot_of == slot_sub
    def select(h):
        ids = nbr[:, h * half:(h + 1) * half]
        shape = (slots, half)
        base = me * (2 * half) + h * half
        diff = ids - base - lax.broadcasted_iota(jnp.int32, shape, 1)
        live = lax.broadcasted_iota(jnp.int32, shape, 0) < cnt[:, h * half:(h + 1) * half]
        diff = jnp.where(live, diff.astype(F32), DEAD).astype(BF)
        z = jnp.where(slot_pick, dot_nt(diff, spread), 0.0)
        row = jnp.sum(z, axis=0, keepdims=True)
        row_t = row + atom_lane[:1] + half
        row_self = jnp.where(row < DEAD / 2, atom_lane[:1], -1.0)
        own_js = (1, 2) if h == 0 else (0, 1)
        rim_j = 0 if h == 0 else 2
        for c in range(0, edges, chunk):
            sub = lax.broadcasted_iota(jnp.int32, (half, chunk), 0).astype(F32)
            rt = row_t[:, c:c + chunk]
            rs = row_self[:, c:c + chunk]
            for pos, j in enumerate(own_js):
                pt_own[pos * half:(pos + 1) * half, h * edges + c:h * edges + c + chunk] = hot(
                    sub + j * half == rt)
            pt_rim[h, :, c:c + chunk] = hot(sub + rim_j * half == rt)
            pt_self[h, :, c:c + chunk] = hot(sub == rs)
        for c in range(0, edges, chunk):
            y = dot_nt(spread[c:c + chunk], diff)
            r8 = lax.broadcasted_iota(jnp.int32, (chunk, slots), 0) % slots
            l8 = lax.broadcasted_iota(jnp.int32, (chunk, slots), 1)
            y = jnp.where(r8 == l8, y, 0.0).astype(BF)
            b = dot(y, jnp.ones((slots, half), BF))
            atom = ((lax.broadcasted_iota(jnp.int32, (chunk, half), 0) + c) // slots).astype(F32)
            col = lax.broadcasted_iota(jnp.int32, (chunk, half), 1).astype(F32)
            ct = b + atom + half
            cs = jnp.where(b < DEAD / 2, atom, -1.0)
            rows = slice(h * edges + c, h * edges + c + chunk)
            for pos, j in enumerate(own_js):
                p_own[rows, pos * half:(pos + 1) * half] = hot(col + j * half == ct)
            p_own[rows, 2 * half:3 * half] = hot(col == cs)
            p_rim[rows] = hot(col + rim_j * half == ct)

    def prepare(h):
        if h == 1:
            loads[4].wait()
        proj[h, 2 * half:3 * half] = dot(feat[h * half:(h + 1) * half], ws[...]).astype(BF)
        if h == 1:
            for i in (5, 6, 7, 8):
                loads[i].wait()

        @pl.loop(0, edges // chunk, unroll=True)
        def _(i):
            rows = pl.ds(pl.multiple_of(h * edges + i * chunk, chunk), chunk)
            g = 0.5 * dot(rad[rows], wr[...])
            gate[rows] = g
            had[rows] = dot_nt(cot[rows], wb[...]) * g
            u_own[rows] = dot(p_own[rows], proj[h])

    def stages(h):
        for c in range(COLS):
            cols = slice(spans[c][0], sum(spans[c]))

            @pl.when(has[h])
            def _():
                halo_copies[1 - h][c].wait_recv()

            rim = None
            for r in range(0, edges, 128):
                rows = slice(h * edges + r, h * edges + r + 128)
                u = u_own[rows, cols] + dot(p_rim[rows], halo[h, :, cols])
                p = u * gate[rows, cols]
                t = jnp.tanh(p)
                pt = p * t
                msg[rows, cols] = (p + pt).astype(BF)
                adjoint = (had[rows, cols] * ((1.0 + t) * ((1.0 + p) - pt))).astype(BF)
                adj[rows, cols] = adjoint
                piece = dot(pt_rim[h, :, r:r + 128], adjoint)
                rim = piece if rim is None else rim + piece
            rim_out[h, :, cols] = rim.astype(BF)

            @pl.when(has[h])
            def _():
                rim_copies[h][c].start()

    def rest(h, first):
        for r in range(0, edges, chunk):
            rows = slice(h * edges + r, h * edges + r + chunk)
            blk[rows] = dot(msg[rows], wb[...]).astype(BF)

        mine = slice(h * edges, (h + 1) * edges)
        own_part = dot(pt_own[:, mine], adj[mine])
        own_sum[...] = own_part if first else own_sum[...] + own_part
        self_adj = dot(pt_self[h], adj[mine]).astype(BF)
        fg_self = fg_part if h == 1 else fg_low
        fg_self[...] = dot_nt(self_adj, ws[...])

    select(1)
    loads[0].wait()
    loads[1].wait()
    own = dot(feat[...], wn[...]).astype(BF)
    for h in (0, 1):
        proj[h, 0:2 * half] = own

    @pl.when(jnp.logical_not(late))
    def _():
        meet()

    for side in (0, 1):
        @pl.when(jnp.logical_not(has[side]))
        def _():
            halo[side] = jnp.zeros_like(halo[side])
            rim_in[side] = jnp.zeros_like(rim_in[side])

    prepare(1)
    @pl.when(late)
    def _():
        meet()

    stages(1)
    select(0)
    prepare(0)
    stages(0)
    rest(1, True)
    rest(0, False)

    for h in (1, 0):
        rows = slice(h * half, (h + 1) * half)
        for c in range(COLS):
            cols = slice(spans[c][0], sum(spans[c]))

            @pl.when(has[h])
            def _():
                rim_copies[1 - h][c].wait_recv()

            total = (own_sum[rows, cols] + rim_in[h, :, cols].astype(F32)).astype(BF)
            if h == 1:
                fg_part[...] += dot_nt(total, wn[:, cols])
            else:
                nbr_adj[:, cols] = total
        if h == 1:
            fg_high[...] = fg_part[...].astype(BF)

    for side in (0, 1):
        @pl.when(has[side])
        def _():
            for copy in halo_copies[side] + rim_copies[side]:
                copy.wait_send()

    @pl.when(relay)
    def _():
        for copy in pass_on:
            copy.wait_send()


def finish_kernel(blk, fg_high, fg_low, nbr_adj, wn, blk_hbm, fg_hbm, fg, sem):
    half = fg.shape[0]
    copies = [
        pltpu.make_async_copy(blk, blk_hbm, sem.at[0]),
        pltpu.make_async_copy(fg_high, fg_hbm.at[pl.ds(half, half)], sem.at[1]),
        pltpu.make_async_copy(fg, fg_hbm.at[pl.ds(0, half)], sem.at[2]),
    ]
    copies[0].start()
    copies[1].start()
    fg[...] = (fg_low[...] + dot_nt(nbr_adj[...], wn[...])).astype(BF)
    copies[2].start()
    for copy in copies:
        copy.wait()


def body(features, radial, neighbours, counts, cotangent, w_self, w_neighbour, w_radial, w_block):
    atoms, width = features.shape
    slots = neighbours.shape[1]
    basis = radial.shape[2]
    out_width = w_block.shape[1]
    half = atoms // 2
    edges = atoms * slots
    n_dev = lax.axis_size("cell")
    any_spec = pl.BlockSpec(memory_space=pl.ANY)
    vm = pltpu.VMEM
    dma = pltpu.SemaphoreType.DMA
    vm_spec = pl.BlockSpec(memory_space=vm)
    parts = pl.pallas_call(
        functools.partial(kernel, n_dev, slots, half, 256),
        name="edge_layer",
        out_shape=(
            vm((edges, out_width), BF), vm((half, width), BF), vm((half, width), F32),
            vm((half, width), BF), vm((width, width), BF),
        ),
        in_specs=[any_spec] * 9,
        out_specs=(vm_spec,) * 5,
        scratch_shapes=[
            vm((atoms, width), BF), vm((edges, basis), BF), vm((slots, atoms), jnp.int32),
            vm((1, atoms), jnp.int32), vm((edges, out_width), BF), vm((width, width), BF),
            vm((basis, width), BF), vm((width, out_width), BF),
            vm((2, half, width), BF), vm((half, width), BF),
            vm((2, half, width), BF), vm((2, half, width), BF),
            vm((2, 3 * half, width), BF),
            vm((edges, 3 * half), BF), vm((edges, half), BF),
            vm((atoms, edges), BF), vm((2, half, edges // 2), BF), vm((2, half, edges // 2), BF),
            vm((edges, width), F32), vm((edges, width), F32), vm((edges, width), F32),
            vm((edges, width), BF), vm((edges, width), BF),
            vm((atoms, width), F32), vm((half, width), F32),
            dma((9,)), dma((2, COLS)), dma((2, COLS)), dma((COLS,)), dma((COLS,)),
            dma((2, COLS)), dma((2, COLS)),
        ],
        compiler_params=pltpu.CompilerParams(
            collective_id=0, has_side_effects=True, vmem_limit_bytes=56 * 1024 * 1024),
    )(
        features, radial.reshape(edges, basis), neighbours.T, counts.reshape(1, atoms),
        cotangent.reshape(edges, out_width), w_self, w_neighbour, w_radial, w_block,
    )
    blocks, grad = pl.pallas_call(
        finish_kernel,
        name="finish",
        out_shape=(
            jax.ShapeDtypeStruct((edges, out_width), BF),
            jax.ShapeDtypeStruct((atoms, width), BF),
        ),
        in_specs=[vm_spec] * 5,
        out_specs=(any_spec, any_spec),
        scratch_shapes=[vm((half, width), BF), dma((3,))],
    )(*[pltpu.with_memory_space_constraint(array, vm) for array in parts])
    return blocks.reshape(atoms, slots, out_width), grad


def solution(mesh):
    in_specs = (
        P("cell", None),
        P("cell", None, None),
        P("cell", None),
        P("cell"),
        P("cell", None, None),
        P(),
        P(),
        P(),
        P(),
    )
    out_specs = (P("cell", None, None), P("cell", None))
    return jax.shard_map(body, mesh=mesh, in_specs=in_specs, out_specs=out_specs, check_vma=False)
```

```python
import functools

import jax
import jax.numpy as jnp
from jax import lax
from jax.experimental import pallas as pl
from jax.experimental.pallas import tpu as pltpu
from jax.sharding import PartitionSpec as P

MESH = pl.DeviceIdType.MESH
BF = jnp.bfloat16
F32 = jnp.float32
DEAD = 1024.0
PARTS = ((0, 4), (4, 4))
COLS = len(PARTS)
ROUND = 128
RELAY = 15
NT = (((1,), (1,)), ((), ()))


def dot(a, b):
    return jnp.dot(a, b, preferred_element_type=F32)


def dot_nt(a, b):
    return lax.dot_general(a, b, NT, preferred_element_type=F32)


def hot(mask):
    return jnp.where(mask, 1.0, 0.0).astype(BF)


def kernel(
    n_dev, slots, half, chunk,
    feat_hbm, rad_hbm, nbr_hbm, cnt_hbm, cot_hbm, ws_hbm, wn_hbm, wr_hbm, wb_hbm,
    blk, fg_high, fg_low, nbr_adj, wn,
    feat, rad, nbr, cnt, cot, ws, wr, wb,
    halo, passed, rim_out, rim_in, proj, p_own, p_rim, pt_own, pt_rim, pt_self,
    gate, had, u_own, msg, adj, own_sum, fg_part,
    in_sem, halo_send, halo_recv, pass_send, pass_recv, rim_send, rim_recv,
):
    me = lax.axis_index("cell")
    has = (me > 0, me < n_dev - 1)
    peer = (me - 1, me + 1)
    spot = lax.rem(me, ROUND)
    far_low = jnp.logical_and(spot == ROUND - 1, has[1])
    far_high = jnp.logical_and(spot == 0, has[0])
    relay = jnp.logical_and(spot == RELAY, me + ROUND < n_dev)
    late = jnp.logical_or(relay, me == 1)
    greet = (me - 1, jnp.where(far_low, me - (ROUND - 1 - RELAY), me + 1))
    edges = half * slots
    width = feat.shape[1]
    spans = [(a * width // 8, n * width // 8) for a, n in PARTS]

    barrier = pltpu.get_barrier_semaphore()
    for side in (1, 0):
        @pl.when(has[side])
        def _():
            pl.semaphore_signal(barrier, inc=1, device_id=(greet[side],), device_id_type=MESH)

    @pl.when(relay)
    def _():
        pl.semaphore_signal(
            barrier, inc=1, device_id=(me + ROUND - RELAY,), device_id_type=MESH)

    pairs = [(feat_hbm, feat), (wn_hbm, wn), (nbr_hbm, nbr), (cnt_hbm, cnt), (ws_hbm, ws),
             (rad_hbm, rad), (wr_hbm, wr), (cot_hbm, cot), (wb_hbm, wb)]
    loads = [pltpu.make_async_copy(s, d, in_sem.at[i]) for i, (s, d) in enumerate(pairs)]
    for load in loads:
        load.start()

    halo_copies = [[
        pltpu.make_async_remote_copy(
            src_ref=proj.at[0, pl.ds(side * half, half), pl.ds(*spans[c])],
            dst_ref=halo.at[1 - side, :, pl.ds(*spans[c])],
            send_sem=halo_send.at[side, c], recv_sem=halo_recv.at[1 - side, c],
            device_id=(peer[side],), device_id_type=MESH)
        for c in range(COLS)] for side in (0, 1)]
    rim_copies = [[
        pltpu.make_async_remote_copy(
            src_ref=rim_out.at[side, :, pl.ds(*spans[c])],
            dst_ref=rim_in.at[1 - side, :, pl.ds(*spans[c])],
            send_sem=rim_send.at[side, c], recv_sem=rim_recv.at[1 - side, c],
            device_id=(peer[side],), device_id_type=MESH)
        for c in range(COLS)] for side in (0, 1)]

    pass_in = [
        pltpu.make_async_remote_copy(
            src_ref=proj.at[0, pl.ds(0, half), pl.ds(*spans[c])], dst_ref=passed.at[:, pl.ds(*spans[c])],
            send_sem=halo_send.at[0, c], recv_sem=pass_recv.at[c],
            device_id=(me - (ROUND - RELAY),), device_id_type=MESH)
        for c in range(COLS)]
    pass_on = [
        pltpu.make_async_remote_copy(
            src_ref=passed.at[:, pl.ds(*spans[c])], dst_ref=halo.at[1, :, pl.ds(*spans[c])],
            send_sem=pass_send.at[c], recv_sem=halo_recv.at[1, c],
            device_id=(me + (ROUND - 1 - RELAY),), device_id_type=MESH)
        for c in range(COLS)]

    def meet():
        count = has[0].astype(jnp.int32) + has[1].astype(jnp.int32) + relay.astype(jnp.int32)
        pl.semaphore_wait(barrier, count)

        @pl.when(relay)
        def _():
            for c in range(COLS):
                pass_in[c].wait_recv()
                pass_on[c].start()

        @pl.when(far_high)
        def _():
            for copy in pass_in:
                copy.start()

        @pl.when(jnp.logical_and(has[0], jnp.logical_not(far_high)))
        def _():
            for copy in halo_copies[0]:
                copy.start()

        @pl.when(has[1])
        def _():
            for copy in halo_copies[1]:
                copy.start()

    loads[2].wait()
    loads[3].wait()
    e_row = lax.broadcasted_iota(jnp.int32, (edges, half), 0)
    lane = lax.broadcasted_iota(jnp.int32, (edges, half), 1)
    spread = hot((e_row // slots) == lane)
    slot_of = lax.broadcasted_iota(jnp.int32, (slots, edges), 1)
    atom_lane = (slot_of // slots).astype(F32)
    slot_of = slot_of % slots
    slot_sub = lax.broadcasted_iota(jnp.int32, (slots, edges), 0)
    slot_pick = slot_of == slot_sub
    def select(h):
        ids = nbr[:, h * half:(h + 1) * half]
        shape = (slots, half)
        base = me * (2 * half) + h * half
        diff = ids - base - lax.broadcasted_iota(jnp.int32, shape, 1)
        live = lax.broadcasted_iota(jnp.int32, shape, 0) < cnt[:, h * half:(h + 1) * half]
        diff = jnp.where(live, diff.astype(F32), DEAD).astype(BF)
        z = jnp.where(slot_pick, dot_nt(diff, spread), 0.0)
        row = jnp.sum(z, axis=0, keepdims=True)
        row_t = row + atom_lane[:1] + half
        row_self = jnp.where(row < DEAD / 2, atom_lane[:1], -1.0)
        own_js = (1, 2) if h == 0 else (0, 1)
        rim_j = 0 if h == 0 else 2
        for c in range(0, edges, chunk):
            sub = lax.broadcasted_iota(jnp.int32, (half, chunk), 0).astype(F32)
            rt = row_t[:, c:c + chunk]
            rs = row_self[:, c:c + chunk]
            for pos, j in enumerate(own_js):
                pt_own[pos * half:(pos + 1) * half, h * edges + c:h * edges + c + chunk] = hot(
                    sub + j * half == rt)
            pt_rim[h, :, c:c + chunk] = hot(sub + rim_j * half == rt)
            pt_self[h, :, c:c + chunk] = hot(sub == rs)
        for c in range(0, edges, chunk):
            y = dot_nt(spread[c:c + chunk], diff)
            r8 = lax.broadcasted_iota(jnp.int32, (chunk, slots), 0) % slots
            l8 = lax.broadcasted_iota(jnp.int32, (chunk, slots), 1)
            y = jnp.where(r8 == l8, y, 0.0).astype(BF)
            b = dot(y, jnp.ones((slots, half), BF))
            atom = ((lax.broadcasted_iota(jnp.int32, (chunk, half), 0) + c) // slots).astype(F32)
            col = lax.broadcasted_iota(jnp.int32, (chunk, half), 1).astype(F32)
            ct = b + atom + half
            cs = jnp.where(b < DEAD / 2, atom, -1.0)
            rows = slice(h * edges + c, h * edges + c + chunk)
            for pos, j in enumerate(own_js):
                p_own[rows, pos * half:(pos + 1) * half] = hot(col + j * half == ct)
            p_own[rows, 2 * half:3 * half] = hot(col == cs)
            p_rim[rows] = hot(col + rim_j * half == ct)

    def prepare(h):
        if h == 1:
            loads[4].wait()
        proj[h, 2 * half:3 * half] = dot(feat[h * half:(h + 1) * half], ws[...]).astype(BF)
        if h == 1:
            for i in (5, 6, 7, 8):
                loads[i].wait()

        @pl.loop(0, edges // chunk, unroll=True)
        def _(i):
            rows = pl.ds(pl.multiple_of(h * edges + i * chunk, chunk), chunk)
            g = 0.5 * dot(rad[rows], wr[...])
            gate[rows] = g
            had[rows] = dot_nt(cot[rows], wb[...]) * g
            u_own[rows] = dot(p_own[rows], proj[h])

    def stages(h):
        for c in range(COLS):
            cols = slice(spans[c][0], sum(spans[c]))

            @pl.when(has[h])
            def _():
                halo_copies[1 - h][c].wait_recv()

            rim = None
            for r in range(0, edges, 128):
                rows = slice(h * edges + r, h * edges + r + 128)
                u = u_own[rows, cols] + dot(p_rim[rows], halo[h, :, cols])
                p = u * gate[rows, cols]
                t = jnp.tanh(p)
                pt = p * t
                msg[rows, cols] = (p + pt).astype(BF)
                adjoint = (had[rows, cols] * ((1.0 + t) * ((1.0 + p) - pt))).astype(BF)
                adj[rows, cols] = adjoint
                piece = dot(pt_rim[h, :, r:r + 128], adjoint)
                rim = piece if rim is None else rim + piece
            rim_out[h, :, cols] = rim.astype(BF)

            @pl.when(has[h])
            def _():
                rim_copies[h][c].start()

    def rest(h, first):
        for r in range(0, edges, chunk):
            rows = slice(h * edges + r, h * edges + r + chunk)
            blk[rows] = dot(msg[rows], wb[...]).astype(BF)

        mine = slice(h * edges, (h + 1) * edges)
        own_part = dot(pt_own[:, mine], adj[mine])
        own_sum[...] = own_part if first else own_sum[...] + own_part
        self_adj = dot(pt_self[h], adj[mine]).astype(BF)
        fg_self = fg_part if h == 1 else fg_low
        fg_self[...] = dot_nt(self_adj, ws[...])

    select(1)
    loads[0].wait()
    loads[1].wait()
    own = dot(feat[...], wn[...]).astype(BF)
    for h in (0, 1):
        proj[h, 0:2 * half] = own

    @pl.when(jnp.logical_not(late))
    def _():
        meet()

    for side in (0, 1):
        @pl.when(jnp.logical_not(has[side]))
        def _():
            halo[side] = jnp.zeros_like(halo[side])
            rim_in[side] = jnp.zeros_like(rim_in[side])

    prepare(1)
    @pl.when(late)
    def _():
        meet()

    stages(1)
    rest(1, True)
    select(0)
    prepare(0)
    stages(0)
    rest(0, False)

    for h in (1, 0):
        rows = slice(h * half, (h + 1) * half)
        for c in range(COLS):
            cols = slice(spans[c][0], sum(spans[c]))

            @pl.when(has[h])
            def _():
                rim_copies[1 - h][c].wait_recv()

            total = (own_sum[rows, cols] + rim_in[h, :, cols].astype(F32)).astype(BF)
            if h == 1:
                fg_part[...] += dot_nt(total, wn[:, cols])
            else:
                nbr_adj[:, cols] = total
        if h == 1:
            fg_high[...] = fg_part[...].astype(BF)

    for side in (0, 1):
        @pl.when(has[side])
        def _():
            for copy in halo_copies[side] + rim_copies[side]:
                copy.wait_send()

    @pl.when(relay)
    def _():
        for copy in pass_on:
            copy.wait_send()


def finish_kernel(blk, fg_high, fg_low, nbr_adj, wn, blk_hbm, fg_hbm, fg, sem):
    half = fg.shape[0]
    copies = [
        pltpu.make_async_copy(blk, blk_hbm, sem.at[0]),
        pltpu.make_async_copy(fg_high, fg_hbm.at[pl.ds(half, half)], sem.at[1]),
        pltpu.make_async_copy(fg, fg_hbm.at[pl.ds(0, half)], sem.at[2]),
    ]
    copies[0].start()
    copies[1].start()
    fg[...] = (fg_low[...] + dot_nt(nbr_adj[...], wn[...])).astype(BF)
    copies[2].start()
    for copy in copies:
        copy.wait()


def body(features, radial, neighbours, counts, cotangent, w_self, w_neighbour, w_radial, w_block):
    atoms, width = features.shape
    slots = neighbours.shape[1]
    basis = radial.shape[2]
    out_width = w_block.shape[1]
    half = atoms // 2
    edges = atoms * slots
    n_dev = lax.axis_size("cell")
    any_spec = pl.BlockSpec(memory_space=pl.ANY)
    vm = pltpu.VMEM
    dma = pltpu.SemaphoreType.DMA
    vm_spec = pl.BlockSpec(memory_space=vm)
    parts = pl.pallas_call(
        functools.partial(kernel, n_dev, slots, half, 256),
        name="edge_layer",
        out_shape=(
            vm((edges, out_width), BF), vm((half, width), BF), vm((half, width), F32),
            vm((half, width), BF), vm((width, width), BF),
        ),
        in_specs=[any_spec] * 9,
        out_specs=(vm_spec,) * 5,
        scratch_shapes=[
            vm((atoms, width), BF), vm((edges, basis), BF), vm((slots, atoms), jnp.int32),
            vm((1, atoms), jnp.int32), vm((edges, out_width), BF), vm((width, width), BF),
            vm((basis, width), BF), vm((width, out_width), BF),
            vm((2, half, width), BF), vm((half, width), BF),
            vm((2, half, width), BF), vm((2, half, width), BF),
            vm((2, 3 * half, width), BF),
            vm((edges, 3 * half), BF), vm((edges, half), BF),
            vm((atoms, edges), BF), vm((2, half, edges // 2), BF), vm((2, half, edges // 2), BF),
            vm((edges, width), F32), vm((edges, width), F32), vm((edges, width), F32),
            vm((edges, width), BF), vm((edges, width), BF),
            vm((atoms, width), F32), vm((half, width), F32),
            dma((9,)), dma((2, COLS)), dma((2, COLS)), dma((COLS,)), dma((COLS,)),
            dma((2, COLS)), dma((2, COLS)),
        ],
        compiler_params=pltpu.CompilerParams(
            collective_id=0, has_side_effects=True, vmem_limit_bytes=56 * 1024 * 1024),
    )(
        features, radial.reshape(edges, basis), neighbours.T, counts.reshape(1, atoms),
        cotangent.reshape(edges, out_width), w_self, w_neighbour, w_radial, w_block,
    )
    blocks, grad = pl.pallas_call(
        finish_kernel,
        name="finish",
        out_shape=(
            jax.ShapeDtypeStruct((edges, out_width), BF),
            jax.ShapeDtypeStruct((atoms, width), BF),
        ),
        in_specs=[vm_spec] * 5,
        out_specs=(any_spec, any_spec),
        scratch_shapes=[vm((half, width), BF), dma((3,))],
    )(*[pltpu.with_memory_space_constraint(array, vm) for array in parts])
    return blocks.reshape(atoms, slots, out_width), grad


def solution(mesh):
    in_specs = (
        P("cell", None),
        P("cell", None, None),
        P("cell", None),
        P("cell"),
        P("cell", None, None),
        P(),
        P(),
        P(),
        P(),
    )
    out_specs = (P("cell", None, None), P("cell", None))
    return jax.shard_map(body, mesh=mesh, in_specs=in_specs, out_specs=out_specs, check_vma=False)
```

```python
import functools

import jax
import jax.numpy as jnp
from jax import lax
from jax.experimental import pallas as pl
from jax.experimental.pallas import tpu as pltpu
from jax.sharding import PartitionSpec as P

MESH = pl.DeviceIdType.MESH
BF = jnp.bfloat16
F32 = jnp.float32
DEAD = 1024.0
PARTS = ((0, 4), (4, 4))
COLS = len(PARTS)
ROUND = 128
RELAY = 15
NT = (((1,), (1,)), ((), ()))


def dot(a, b):
    return jnp.dot(a, b, preferred_element_type=F32)


def dot_nt(a, b):
    return lax.dot_general(a, b, NT, preferred_element_type=F32)


def hot(mask):
    return jnp.where(mask, 1.0, 0.0).astype(BF)


def kernel(
    n_dev, slots, half, chunk,
    feat_hbm, rad_hbm, nbr_hbm, cnt_hbm, cot_hbm, ws_hbm, wn_hbm, wr_hbm, wb_hbm,
    blk, fg_high, fg_low, nbr_adj, wn,
    feat, rad, nbr, cnt, cot, ws, wr, wb,
    halo, passed, rim_out, rim_in, proj, p_own, p_rim, pt_own, pt_rim, pt_self,
    gate, had, u_own, msg, adj, own_sum, fg_part,
    in_sem, halo_send, halo_recv, pass_send, pass_recv, rim_send, rim_recv,
):
    me = lax.axis_index("cell")
    has = (me > 0, me < n_dev - 1)
    peer = (me - 1, me + 1)
    spot = lax.rem(me, ROUND)
    far_low = jnp.logical_and(spot == ROUND - 1, has[1])
    far_high = jnp.logical_and(spot == 0, has[0])
    relay = jnp.logical_and(spot == RELAY, me + ROUND < n_dev)
    late = jnp.logical_or(relay, me == 1)
    greet = (me - 1, jnp.where(far_low, me - (ROUND - 1 - RELAY), me + 1))
    edges = half * slots
    width = feat.shape[1]
    spans = [(a * width // 8, n * width // 8) for a, n in PARTS]

    barrier = pltpu.get_barrier_semaphore()
    for side in (1, 0):
        @pl.when(has[side])
        def _():
            pl.semaphore_signal(barrier, inc=1, device_id=(greet[side],), device_id_type=MESH)

    @pl.when(relay)
    def _():
        pl.semaphore_signal(
            barrier, inc=1, device_id=(me + ROUND - RELAY,), device_id_type=MESH)

    pairs = [(feat_hbm, feat), (wn_hbm, wn), (nbr_hbm, nbr), (cnt_hbm, cnt), (ws_hbm, ws),
             (rad_hbm, rad), (wr_hbm, wr), (cot_hbm, cot), (wb_hbm, wb)]
    loads = [pltpu.make_async_copy(s, d, in_sem.at[i]) for i, (s, d) in enumerate(pairs)]
    for load in loads:
        load.start()

    halo_copies = [[
        pltpu.make_async_remote_copy(
            src_ref=proj.at[0, pl.ds(side * half, half), pl.ds(*spans[c])],
            dst_ref=halo.at[1 - side, :, pl.ds(*spans[c])],
            send_sem=halo_send.at[side, c], recv_sem=halo_recv.at[1 - side, c],
            device_id=(peer[side],), device_id_type=MESH)
        for c in range(COLS)] for side in (0, 1)]
    rim_copies = [[
        pltpu.make_async_remote_copy(
            src_ref=rim_out.at[side, :, pl.ds(*spans[c])],
            dst_ref=rim_in.at[1 - side, :, pl.ds(*spans[c])],
            send_sem=rim_send.at[side, c], recv_sem=rim_recv.at[1 - side, c],
            device_id=(peer[side],), device_id_type=MESH)
        for c in range(COLS)] for side in (0, 1)]

    pass_in = [
        pltpu.make_async_remote_copy(
            src_ref=proj.at[0, pl.ds(0, half), pl.ds(*spans[c])], dst_ref=passed.at[:, pl.ds(*spans[c])],
            send_sem=halo_send.at[0, c], recv_sem=pass_recv.at[c],
            device_id=(me - (ROUND - RELAY),), device_id_type=MESH)
        for c in range(COLS)]
    pass_on = [
        pltpu.make_async_remote_copy(
            src_ref=passed.at[:, pl.ds(*spans[c])], dst_ref=halo.at[1, :, pl.ds(*spans[c])],
            send_sem=pass_send.at[c], recv_sem=halo_recv.at[1, c],
            device_id=(me + (ROUND - 1 - RELAY),), device_id_type=MESH)
        for c in range(COLS)]

    def meet():
        count = has[0].astype(jnp.int32) + has[1].astype(jnp.int32) + relay.astype(jnp.int32)
        pl.semaphore_wait(barrier, count)

        @pl.when(relay)
        def _():
            for c in range(COLS):
                pass_in[c].wait_recv()
                pass_on[c].start()

        @pl.when(has[1])
        def _():
            for copy in halo_copies[1]:
                copy.start()

        @pl.when(far_high)
        def _():
            for copy in pass_in:
                copy.start()

        @pl.when(jnp.logical_and(has[0], jnp.logical_not(far_high)))
        def _():
            for copy in halo_copies[0]:
                copy.start()

    loads[2].wait()
    loads[3].wait()
    e_row = lax.broadcasted_iota(jnp.int32, (edges, half), 0)
    lane = lax.broadcasted_iota(jnp.int32, (edges, half), 1)
    spread = hot((e_row // slots) == lane)
    slot_of = lax.broadcasted_iota(jnp.int32, (slots, edges), 1)
    atom_lane = (slot_of // slots).astype(F32)
    slot_of = slot_of % slots
    slot_sub = lax.broadcasted_iota(jnp.int32, (slots, edges), 0)
    slot_pick = slot_of == slot_sub
    def select(h):
        ids = nbr[:, h * half:(h + 1) * half]
        shape = (slots, half)
        base = me * (2 * half) + h * half
        diff = ids - base - lax.broadcasted_iota(jnp.int32, shape, 1)
        live = lax.broadcasted_iota(jnp.int32, shape, 0) < cnt[:, h * half:(h + 1) * half]
        diff = jnp.where(live, diff.astype(F32), DEAD).astype(BF)
        z = jnp.where(slot_pick, dot_nt(diff, spread), 0.0)
        row = jnp.sum(z, axis=0, keepdims=True)
        row_t = row + atom_lane[:1] + half
        row_self = jnp.where(row < DEAD / 2, atom_lane[:1], -1.0)
        own_js = (1, 2) if h == 0 else (0, 1)
        rim_j = 0 if h == 0 else 2
        for c in range(0, edges, chunk):
            sub = lax.broadcasted_iota(jnp.int32, (half, chunk), 0).astype(F32)
            rt = row_t[:, c:c + chunk]
            rs = row_self[:, c:c + chunk]
            for pos, j in enumerate(own_js):
                pt_own[pos * half:(pos + 1) * half, h * edges + c:h * edges + c + chunk] = hot(
                    sub + j * half == rt)
            pt_rim[h, :, c:c + chunk] = hot(sub + rim_j * half == rt)
            pt_self[h, :, c:c + chunk] = hot(sub == rs)
        for c in range(0, edges, chunk):
            y = dot_nt(spread[c:c + chunk], diff)
            r8 = lax.broadcasted_iota(jnp.int32, (chunk, slots), 0) % slots
            l8 = lax.broadcasted_iota(jnp.int32, (chunk, slots), 1)
            y = jnp.where(r8 == l8, y, 0.0).astype(BF)
            b = dot(y, jnp.ones((slots, half), BF))
            atom = ((lax.broadcasted_iota(jnp.int32, (chunk, half), 0) + c) // slots).astype(F32)
            col = lax.broadcasted_iota(jnp.int32, (chunk, half), 1).astype(F32)
            ct = b + atom + half
            cs = jnp.where(b < DEAD / 2, atom, -1.0)
            rows = slice(h * edges + c, h * edges + c + chunk)
            for pos, j in enumerate(own_js):
                p_own[rows, pos * half:(pos + 1) * half] = hot(col + j * half == ct)
            p_own[rows, 2 * half:3 * half] = hot(col == cs)
            p_rim[rows] = hot(col + rim_j * half == ct)

    def prepare(h):
        if h == 1:
            loads[4].wait()
        proj[h, 2 * half:3 * half] = dot(feat[h * half:(h + 1) * half], ws[...]).astype(BF)
        if h == 1:
            for i in (5, 6, 7, 8):
                loads[i].wait()

        @pl.loop(0, edges // chunk, unroll=True)
        def _(i):
            rows = pl.ds(pl.multiple_of(h * edges + i * chunk, chunk), chunk)
            g = 0.5 * dot(rad[rows], wr[...])
            gate[rows] = g
            had[rows] = dot_nt(cot[rows], wb[...]) * g
            u_own[rows] = dot(p_own[rows], proj[h])

    def stages(h):
        for c in range(COLS):
            cols = slice(spans[c][0], sum(spans[c]))

            @pl.when(has[h])
            def _():
                halo_copies[1 - h][c].wait_recv()

            rim = None
            for r in range(0, edges, 128):
                rows = slice(h * edges + r, h * edges + r + 128)
                u = u_own[rows, cols] + dot(p_rim[rows], halo[h, :, cols])
                p = u * gate[rows, cols]
                t = jnp.tanh(p)
                pt = p * t
                msg[rows, cols] = (p + pt).astype(BF)
                adjoint = (had[rows, cols] * ((1.0 + t) * ((1.0 + p) - pt))).astype(BF)
                adj[rows, cols] = adjoint
                piece = dot(pt_rim[h, :, r:r + 128], adjoint)
                rim = piece if rim is None else rim + piece
            rim_out[h, :, cols] = rim.astype(BF)

            @pl.when(has[h])
            def _():
                rim_copies[h][c].start()

    def rest(h, first):
        for r in range(0, edges, chunk):
            rows = slice(h * edges + r, h * edges + r + chunk)
            blk[rows] = dot(msg[rows], wb[...]).astype(BF)

        mine = slice(h * edges, (h + 1) * edges)
        own_part = dot(pt_own[:, mine], adj[mine])
        own_sum[...] = own_part if first else own_sum[...] + own_part
        self_adj = dot(pt_self[h], adj[mine]).astype(BF)
        fg_self = fg_part if h == 1 else fg_low
        fg_self[...] = dot_nt(self_adj, ws[...])

    select(1)
    loads[0].wait()
    loads[1].wait()
    own = dot(feat[...], wn[...]).astype(BF)
    for h in (0, 1):
        proj[h, 0:2 * half] = own

    @pl.when(jnp.logical_not(late))
    def _():
        meet()

    for side in (0, 1):
        @pl.when(jnp.logical_not(has[side]))
        def _():
            halo[side] = jnp.zeros_like(halo[side])
            rim_in[side] = jnp.zeros_like(rim_in[side])

    prepare(1)
    @pl.when(late)
    def _():
        meet()

    stages(1)
    rest(1, True)
    select(0)
    prepare(0)
    stages(0)
    rest(0, False)

    for h in (1, 0):
        rows = slice(h * half, (h + 1) * half)
        for c in range(COLS):
            cols = slice(spans[c][0], sum(spans[c]))

            @pl.when(has[h])
            def _():
                rim_copies[1 - h][c].wait_recv()

            total = (own_sum[rows, cols] + rim_in[h, :, cols].astype(F32)).astype(BF)
            if h == 1:
                fg_part[...] += dot_nt(total, wn[:, cols])
            else:
                nbr_adj[:, cols] = total
        if h == 1:
            fg_high[...] = fg_part[...].astype(BF)

    for side in (0, 1):
        @pl.when(has[side])
        def _():
            for copy in halo_copies[side] + rim_copies[side]:
                copy.wait_send()

    @pl.when(relay)
    def _():
        for copy in pass_on:
            copy.wait_send()


def finish_kernel(blk, fg_high, fg_low, nbr_adj, wn, blk_hbm, fg_hbm, fg, sem):
    half = fg.shape[0]
    copies = [
        pltpu.make_async_copy(blk, blk_hbm, sem.at[0]),
        pltpu.make_async_copy(fg_high, fg_hbm.at[pl.ds(half, half)], sem.at[1]),
        pltpu.make_async_copy(fg, fg_hbm.at[pl.ds(0, half)], sem.at[2]),
    ]
    copies[0].start()
    copies[1].start()
    fg[...] = (fg_low[...] + dot_nt(nbr_adj[...], wn[...])).astype(BF)
    copies[2].start()
    for copy in copies:
        copy.wait()


def body(features, radial, neighbours, counts, cotangent, w_self, w_neighbour, w_radial, w_block):
    atoms, width = features.shape
    slots = neighbours.shape[1]
    basis = radial.shape[2]
    out_width = w_block.shape[1]
    half = atoms // 2
    edges = atoms * slots
    n_dev = lax.axis_size("cell")
    any_spec = pl.BlockSpec(memory_space=pl.ANY)
    vm = pltpu.VMEM
    dma = pltpu.SemaphoreType.DMA
    vm_spec = pl.BlockSpec(memory_space=vm)
    parts = pl.pallas_call(
        functools.partial(kernel, n_dev, slots, half, 256),
        name="edge_layer",
        out_shape=(
            vm((edges, out_width), BF), vm((half, width), BF), vm((half, width), F32),
            vm((half, width), BF), vm((width, width), BF),
        ),
        in_specs=[any_spec] * 9,
        out_specs=(vm_spec,) * 5,
        scratch_shapes=[
            vm((atoms, width), BF), vm((edges, basis), BF), vm((slots, atoms), jnp.int32),
            vm((1, atoms), jnp.int32), vm((edges, out_width), BF), vm((width, width), BF),
            vm((basis, width), BF), vm((width, out_width), BF),
            vm((2, half, width), BF), vm((half, width), BF),
            vm((2, half, width), BF), vm((2, half, width), BF),
            vm((2, 3 * half, width), BF),
            vm((edges, 3 * half), BF), vm((edges, half), BF),
            vm((atoms, edges), BF), vm((2, half, edges // 2), BF), vm((2, half, edges // 2), BF),
            vm((edges, width), F32), vm((edges, width), F32), vm((edges, width), F32),
            vm((edges, width), BF), vm((edges, width), BF),
            vm((atoms, width), F32), vm((half, width), F32),
            dma((9,)), dma((2, COLS)), dma((2, COLS)), dma((COLS,)), dma((COLS,)),
            dma((2, COLS)), dma((2, COLS)),
        ],
        compiler_params=pltpu.CompilerParams(
            collective_id=0, has_side_effects=True, vmem_limit_bytes=56 * 1024 * 1024),
    )(
        features, radial.reshape(edges, basis), neighbours.T, counts.reshape(1, atoms),
        cotangent.reshape(edges, out_width), w_self, w_neighbour, w_radial, w_block,
    )
    blocks, grad = pl.pallas_call(
        finish_kernel,
        name="finish",
        out_shape=(
            jax.ShapeDtypeStruct((edges, out_width), BF),
            jax.ShapeDtypeStruct((atoms, width), BF),
        ),
        in_specs=[vm_spec] * 5,
        out_specs=(any_spec, any_spec),
        scratch_shapes=[vm((half, width), BF), dma((3,))],
    )(*[pltpu.with_memory_space_constraint(array, vm) for array in parts])
    return blocks.reshape(atoms, slots, out_width), grad


def solution(mesh):
    in_specs = (
        P("cell", None),
        P("cell", None, None),
        P("cell", None),
        P("cell"),
        P("cell", None, None),
        P(),
        P(),
        P(),
        P(),
    )
    out_specs = (P("cell", None, None), P("cell", None))
    return jax.shard_map(body, mesh=mesh, in_specs=in_specs, out_specs=out_specs, check_vma=False)
```
